512 devices in a mesh: gr: 16 (over y, core), gc: 32 (over z, x).
Axes of the slice: x: 4, y: 8, z: 8, core: 2. Of those that a mesh axis runs over, the one named last changes fastest.
Arguments:
- weights: bfloat16 [8192, 8192], P('gc', 'gr'), may hold values from 0.049804688 to 5
- in_pattern: int32 [64, 64], P('gc', 'gr'), may hold values from 0 to 1, as said below
- out_pattern: int32 [64, 64], P('gc', 'gr'), may hold values from 0 to 1, as said below
Outputs:
- next_matrix: bfloat16 [8192, 8192], P('gc', 'gr')
The draws below stay inside these ranges and needn't reach their ends.
Inputs may be any that keep to these rules, and one draw needn't show every extreme that they name: `in_pattern`: 0 or 1 a block; every diagonal block is 1; each aligned tile of 2 block rows by 4 block columns holds at most 4 ones, and one such tile holds exactly 4. `out_pattern`: 0 or 1 a block; every diagonal block is 1.
All inputs are finite; a program needn't handle non-finite values.
Results may differ from the reference program's by a relative error of at most 0.0055.
Values may be sent and summed in bfloat16 or wider, within the bound.
A program may use at most 128 MiB of HBM per device.

```python
import math
import jax
import jax.numpy as jnp
from jax import lax

BLK = 128
BR_DEV = 2
BC_DEV = 4
CAP = 4
N = 8192
NB = 64


def draw_in_pattern(key, part):
    key_scores, key_counts, key_whole = jax.random.split(jax.random.fold_in(key, 11), 3)
    row_ids = jnp.arange(NB, dtype=jnp.int32)[:, None]
    col_ids = jnp.arange(NB, dtype=jnp.int32)[None, :]
    diagonal = row_ids == col_ids
    scores = jax.random.randint(key_scores, (NB, NB), 0, 1 << 20)
    scores = jnp.where(diagonal, -1, scores)
    tile_rows = NB // BR_DEV
    tile_cols = NB // BC_DEV
    within = BR_DEV * BC_DEV
    tiled_scores = scores.reshape(tile_rows, BR_DEV, tile_cols, BC_DEV).transpose(0, 2, 1, 3).reshape(tile_rows, tile_cols, within)
    forced = diagonal.astype(jnp.int32).reshape(tile_rows, BR_DEV, tile_cols, BC_DEV).sum(axis=(1, 3))
    ordinal = jnp.argsort(jnp.argsort(tiled_scores, axis=-1, stable=True), axis=-1, stable=True)
    counts = jax.random.randint(key_counts, (tile_rows, tile_cols), 0, CAP + 1)
    counts = jnp.maximum(counts, forced)
    whole_tile = jax.random.randint(key_whole, (), 0, tile_rows * tile_cols)
    tile_numbers = jnp.arange(tile_rows * tile_cols, dtype=jnp.int32).reshape(tile_rows, tile_cols)
    counts = jnp.where(tile_numbers == whole_tile, CAP, counts)
    block_flags = (ordinal < counts[:, :, None]).astype(jnp.int32)
    return block_flags.reshape(tile_rows, tile_cols, BR_DEV, BC_DEV).transpose(0, 2, 1, 3).reshape(NB, NB)


def draw_out_pattern(key, part):
    row_ids = jnp.arange(NB, dtype=jnp.int32)[:, None]
    col_ids = jnp.arange(NB, dtype=jnp.int32)[None, :]
    keeping = jax.random.randint(jax.random.fold_in(key, 23), (NB, NB), 0, 3) > 0
    return jnp.logical_or(keeping, row_ids == col_ids).astype(jnp.int32)


def block_scale(key, extent, cuts, smallest, top_value):
    loudness, own = 1.0, jax.random.fold_in(key, 6)
    for axis_at, shards_of in cuts:
        steps = jnp.exp(jax.random.uniform(jax.random.fold_in(own, axis_at), (shards_of,), jnp.float32, smallest / len(cuts), top_value / len(cuts)))
        loudness = loudness * jnp.repeat(steps, extent[axis_at] // shards_of).reshape([-1 if axis == axis_at else 1 for axis in range(len(extent))])
    return loudness


def setup_inputs(seed: int = 0) -> dict:
    streams_of = jax.random.split(jax.random.key(seed), 4)
    weights = jnp.clip(jnp.exp(math.log(5.0) - 4.609084 * jax.random.uniform(streams_of[0], (N, N), jnp.float32) ** block_scale(streams_of[0], (N, N), ((0, 32), (1, 16)), -0.2, 0.2)), 0.049804688, 5.0).astype(jnp.bfloat16)
    in_pattern = draw_in_pattern(jax.random.fold_in(streams_of[3], 71), 0)
    out_pattern = draw_out_pattern(jax.random.fold_in(streams_of[3], 71), 0)
    return {"weights": weights, "in_pattern": in_pattern, "out_pattern": out_pattern}


def expand_flags(block_flags):
    return jnp.repeat(jnp.repeat(block_flags, BLK, axis=0), BLK, axis=1)


def reference(weights, in_pattern, out_pattern):
    masked = weights * expand_flags(in_pattern).astype(jnp.bfloat16)
    input_total = jnp.sum(masked.astype(jnp.float32), axis=0)
    inverse = 1.0 / input_total
    stochastic = (masked.astype(jnp.float32) * inverse[None, :]).astype(jnp.bfloat16)
    wide_copy = stochastic.astype(jnp.float32)
    expanded = jnp.dot(wide_copy, wide_copy, precision=lax.Precision.HIGHEST, preferred_element_type=jnp.float32)
    pruned = expanded * expand_flags(out_pattern).astype(jnp.float32)
    inflated = pruned * pruned
    output_total = jnp.sum(inflated, axis=0)
    return ((inflated / output_total[None, :]) * float(N)).astype(jnp.bfloat16)
```

```python
import functools

import jax
import jax.numpy as jnp
from jax import lax
from jax.experimental import pallas as pl
from jax.experimental.pallas import tpu as pltpu
from jax.sharding import PartitionSpec as P

MESH = pl.DeviceIdType.MESH
X = 4
CORES = 2
CAP = 4
SUM_SCALE = float(1 << 14)
CODE_ROW = 4


def kernel(
    gc, gr, blk,
    w_ref, ip_ref, op_ref, o_ref,
    bbuf, abuf, bdense, adense, acc, meta_b, meta_a, totals,
    z_recv, x_recv, y_recv, sib_recv, small_recv, send_sem,
):
    br, bc = ip_ref.shape
    z_chips, y_chips = gc // X, gr // CORES
    tile = CAP * blk
    part = tile // 2
    half = part // 2
    f32, bf16 = jnp.float32, jnp.bfloat16

    me = lax.axis_index("gc")
    mine = lax.axis_index("gr")
    x, z = lax.rem(me, X), lax.div(me, X)
    core, y = lax.rem(mine, CORES), lax.div(mine, CORES)

    def at(dx, dz):
        return lax.rem(z + dz + z_chips, z_chips) * X + lax.rem(x + dx + X, X)

    def at_y(dy, c):
        return lax.rem(y + dy + y_chips, y_chips) * CORES + c

    barrier = pltpu.get_barrier_semaphore()

    @pl.loop(1, gc)
    def _(j):
        pl.semaphore_signal(barrier, inc=1, device_id={"gc": lax.rem(me + j, gc)}, device_id_type=MESH)

    @pl.loop(1, gr)
    def _(j):
        pl.semaphore_signal(barrier, inc=1, device_id={"gr": lax.rem(mine + j, gr)}, device_id_type=MESH)

    def rows(origin):
        return pl.multiple_of(origin * tile, tile)

    spots = br * bc
    on = [(ip_ref[p // bc, p % bc] > 0).astype(jnp.int32) for p in range(spots)]
    spare = CAP - sum(on)
    count = jnp.int32(0)
    place = [jnp.int32(0)] * CAP
    for p in range(spots):
        filler = jnp.logical_and(on[p] == 0, spare > 0).astype(jnp.int32)
        spare = spare - filler
        used = on[p] + filler
        for s in range(CAP):
            place[s] = place[s] + jnp.where(count == s, used, 0) * p
        count = count + used

    def reach(p):
        return range(max(0, p - (spots - CAP)), min(CAP - 1, p) + 1)

    def block_of(p):
        r, c = p // bc, p % bc
        return w_ref[r * blk : (r + 1) * blk, c * blk : (c + 1) * blk]

    for s in range(CAP):
        slot = jnp.zeros((blk, blk), f32)
        for p in range(s, s + spots - CAP + 1):
            slot += block_of(p).astype(f32) * (jnp.where(place[s] == p, on[p], 0).astype(f32))
        bbuf[pl.ds(rows(me) + s * blk, blk), :] = slot.astype(bf16)

    for c in range(bc):
        total = jnp.zeros((1, blk), f32)
        for r in range(br):
            block = block_of(r * bc + c).astype(f32)
            total += jnp.sum(block, axis=0, keepdims=True) * on[r * bc + c].astype(f32)
        row = (total * SUM_SCALE).astype(jnp.int32)
        meta_b[me, c : c + 1, :] = row
        meta_a[mine, c : c + 1, :] = row
    for s in range(CAP):
        row = jnp.full((1, blk), 0, jnp.int32) + place[s]
        meta_b[me, CODE_ROW + s : CODE_ROW + s + 1, :] = row
        meta_a[mine, CODE_ROW + s : CODE_ROW + s + 1, :] = row

    pl.semaphore_wait(barrier, gc + gr - 2)

    P_ROWS, Q_ROWS, HALF = 0, part, half

    def b_copy(origin, first, size, dst, recv):
        ref = bbuf.at[pl.ds(rows(origin) + first, size), :]
        return pltpu.make_async_remote_copy(
            src_ref=ref, dst_ref=ref, send_sem=send_sem.at[0], recv_sem=recv,
            device_id={"gc": dst}, device_id_type=MESH,
        )

    z_half = z_chips // 2
    Q = X

    def z_copy(s, h, item):
        sign = 1 - 2 * s
        origin = at(0 if item == Q else item, -sign * (h - 1))
        first = Q_ROWS if item == Q else P_ROWS
        size = part
        if h == z_half:
            first, size = first + s * HALF, HALF
        return b_copy(origin, first, size, at(0, sign), z_recv.at[s, h - 1, item])

    PX = z_chips

    def x_copy(d, k, item):
        sign = 1 - 2 * d
        origin = at(-sign * (k - 1), 0 if item == PX else item)
        first = P_ROWS if item == PX else Q_ROWS
        size = part
        if k == X // 2:
            first, size = first + d * HALF, HALF
        return b_copy(origin, first, size, at(sign, 0), x_recv.at[d, k - 1, item])

    def small(ref, index, axis, peer, k):
        return pltpu.make_async_remote_copy(
            src_ref=ref.at[index], dst_ref=ref.at[index], send_sem=send_sem.at[k], recv_sem=small_recv.at[k - 2],
            device_id={axis: peer}, device_id_type=MESH,
        )

    def all_small(ref, n, axis, k):
        view = ref.at[pl.ds(0, n - 1)]
        return pltpu.make_async_remote_copy(
            src_ref=view, dst_ref=view, send_sem=send_sem.at[k], recv_sem=small_recv.at[k - 2],
            device_id={axis: 0}, device_id_type=MESH,
        )

    y_half = y_chips // 2

    def a_copy(origin, first, size, dst, recv):
        ref = abuf.at[pl.ds(rows(origin) + first, size), :]
        return pltpu.make_async_remote_copy(
            src_ref=ref, dst_ref=ref, send_sem=send_sem.at[1], recv_sem=recv,
            device_id={"gr": dst}, device_id_type=MESH,
        )

    def y_copy(s, h):
        sign = 1 - 2 * s
        first, size = (s * part, part) if h == y_half else (0, tile)
        return a_copy(at_y(-sign * (h - 1), core), first, size, at_y(sign, core), y_recv.at[s, h - 1])

    def sib_copy(dy, c):
        return a_copy(at_y(dy, c), 0, tile, at_y(0, 1 - c), sib_recv.at[dy % y_chips])

    for s in range(2):
        z_copy(s, 1, Q).start()
    for d in range(2):
        x_copy(d, 1, PX).start()
    for s in range(2):
        z_copy(s, 1, 0).start()
    for d in range(2):
        x_copy(d, 1, 0).start()

    @pl.loop(1, gc)
    def _(j):
        small(meta_b, me, "gc", lax.rem(me + j, gc), 2).start()

    @pl.loop(1, gr)
    def _(j):
        small(meta_a, mine, "gr", lax.rem(mine + j, gr), 3).start()

    for d in range(2):
        x_copy(d, 1, PX).wait_recv()
        x_copy(d, 2, PX).start()
        for s in range(2):
            z_copy(s, 1, (X - 1) if d == 0 else 1).start()
    for d in range(2):
        x_copy(d, 2, PX).wait_recv()
    for s in range(2):
        z_copy(s, 1, X // 2).start()

    all_small(meta_b, gc, "gc", 2).wait_recv()
    input_total = jnp.sum(meta_b[...], axis=0).astype(f32) * (1.0 / SUM_SCALE)
    inverse = 1.0 / input_total
    for s in range(CAP):
        factor = jnp.zeros((1, blk), f32)
        for c in range(bc):
            factor += inverse[c : c + 1, :] * (lax.rem(place[s], bc) == c).astype(f32)
        block = bbuf[pl.ds(rows(me) + s * blk, blk), :].astype(f32)
        abuf[pl.ds(rows(mine) + s * blk, blk), :] = (block * factor).astype(bf16)
    for s in range(2):
        y_copy(s, 1).start()
    sib_copy(0, core).start()

    for d in range(2):
        x_copy(d, 1, 0).wait_recv()
        x_copy(d, 2, 0).start()

    for h in range(1, z_half + 1):
        last = h == z_half
        for s in range(2):
            z_copy(s, h, Q).wait_recv()
            if not last:
                z_copy(s, h + 1, Q).start()
                for d in range(2):
                    x_copy(d, 1, (-h if s == 0 else h) % z_chips).start()
        if last:
            for d in range(2):
                x_copy(d, 1, h).start()
        for item in (0, 1, X - 1, X // 2):
            for s in range(2):
                z_copy(s, h, item).wait_recv()
                if not last:
                    z_copy(s, h + 1, item).start()
        if h <= y_half:
            for s in range(2):
                y_copy(s, h).wait_recv()
                if h < y_half:
                    y_copy(s, h + 1).start()
                    sib_copy(-h if s == 0 else h, core).start()
            if h == y_half:
                sib_copy(h, core).start()
        for dz in (h % z_chips, -h % z_chips) if not last else (h,):
            for d in range(2):
                x_copy(d, 1, dz).wait_recv()
                x_copy(d, 2, dz).start()
    for dz in range(z_chips):
        for d in range(2):
            x_copy(d, 2, dz).wait_recv()
    for dy in range(y_chips):
        sib_copy(dy, 1 - core).wait_recv()

    all_small(meta_a, gr, "gr", 3).wait_recv()

    def spread(t, meta, buf, dst, r_base):
        slots = [buf[pl.ds(rows(t) + s * blk, blk), :] for s in range(CAP)]
        places = [meta[t, CODE_ROW + s : CODE_ROW + s + 1, :] for s in range(CAP)]
        for p in range(spots):
            block = sum(slots[s] * (places[s] == p).astype(f32).astype(bf16) for s in reach(p))
            r, c = p // bc, p % bc
            dst[pl.ds(r_base + r * blk, blk), c * blk : (c + 1) * blk] = block

    per = (bc * blk) // (br * blk)

    @pl.loop(0, gr)
    def _(t):
        spread(t, meta_a, abuf, adense.at[t], 0)
        for i in range(per):
            spread(t * per + i, meta_b, bbuf, bdense.at[t], i * br * blk)

    acc[...] = jnp.zeros_like(acc)

    @pl.loop(0, gr)
    def _(t):
        acc[...] += jnp.dot(adense[t], bdense[t], preferred_element_type=f32)

    for c in range(bc):
        total = jnp.zeros((1, blk), f32)
        for r in range(br):
            block = acc[r * blk : (r + 1) * blk, c * blk : (c + 1) * blk] * op_ref[r, c].astype(f32)
            block = block * block
            acc[r * blk : (r + 1) * blk, c * blk : (c + 1) * blk] = block
            total += jnp.sum(block, axis=0, keepdims=True)
        totals[me, c : c + 1, :] = total

    @pl.loop(1, gc)
    def _(j):
        small(totals, me, "gc", lax.rem(me + j, gc), 4).start()

    all_small(totals, gc, "gc", 4).wait_recv()
    output_total = jnp.sum(totals[...], axis=0)
    factor = float(gc * br * blk) / output_total
    for c in range(bc):
        o_ref[:, c * blk : (c + 1) * blk] = (acc[:, c * blk : (c + 1) * blk] * factor[c : c + 1, :]).astype(bf16)

    b_copy(0, 0, (gc - 1) * tile, 0, z_recv.at[0, 0, 0]).wait_send()
    a_copy(0, 0, (gr - 1) * tile, 0, y_recv.at[0, 0]).wait_send()
    all_small(meta_b, gc, "gc", 2).wait_send()
    all_small(meta_a, gr, "gr", 3).wait_send()
    all_small(totals, gc, "gc", 4).wait_send()


def solution(mesh):
    gc, gr = mesh.shape["gc"], mesh.shape["gr"]

    def shards(weights, in_pattern, out_pattern):
        rows, cols = weights.shape
        br, bc = in_pattern.shape
        blk = rows // br
        tile = CAP * blk
        z_chips, y_chips = gc // X, gr // CORES
        dma = pltpu.SemaphoreType.DMA
        return pl.pallas_call(
            functools.partial(kernel, gc, gr, blk),
            out_shape=jax.ShapeDtypeStruct(weights.shape, weights.dtype),
            in_specs=[
                pl.BlockSpec(memory_space=pltpu.VMEM),
                pl.BlockSpec(memory_space=pltpu.SMEM),
                pl.BlockSpec(memory_space=pltpu.SMEM),
            ],
            out_specs=pl.BlockSpec(memory_space=pltpu.VMEM),
            scratch_shapes=[
                pltpu.VMEM((gc * tile, blk), jnp.bfloat16),
                pltpu.VMEM((gr * tile, blk), jnp.bfloat16),
                pltpu.VMEM((gr, cols, cols), jnp.bfloat16),
                pltpu.VMEM((gr, rows, cols), jnp.bfloat16),
                pltpu.VMEM((rows, cols), jnp.float32),
                pltpu.VMEM((gc, 8, blk), jnp.int32),
                pltpu.VMEM((gr, 8, blk), jnp.int32),
                pltpu.VMEM((gc, bc, blk), jnp.float32),
                dma((2, z_chips // 2, X + 1)),
                dma((2, X // 2, z_chips + 1)),
                dma((2, y_chips // 2)),
                dma((y_chips,)),
                dma((3,)),
                dma((5,)),
            ],
            compiler_params=pltpu.CompilerParams(
                collective_id=0, has_side_effects=True, vmem_limit_bytes=48 << 20
            ),
        )(weights, in_pattern, out_pattern)

    spec = P("gc", "gr")
    return jax.shard_map(shards, mesh=mesh, in_specs=(spec, spec, spec), out_specs=spec, check_vma=False)
```

```python
import functools

import jax
import jax.numpy as jnp
from jax import lax
from jax.experimental import pallas as pl
from jax.experimental.pallas import tpu as pltpu
from jax.sharding import PartitionSpec as P

MESH = pl.DeviceIdType.MESH
X = 4
CORES = 2
CAP = 4
CODE = 16
P_ROWS = 208


def kernel(
    gc, gr, blk,
    w_hbm, ip_hbm, op_hbm, o_ref,
    w_ref, ip_ref, op_ref, bbuf, abuf, bdense, adense, acc, x_sums, z_sums, inverses, totals,
    z_recv, x_recv, y_recv, sib_recv, small_recv, send_sem, local_sem,
):
    br, bc = ip_ref.shape
    z_chips, y_chips = gc // X, gr // CORES
    x_half, y_half, z_half = X // 2, y_chips // 2, z_chips // 2
    data = CAP * blk
    tile = data + CODE
    f32, bf16 = jnp.float32, jnp.bfloat16

    me = lax.axis_index("gc")
    mine = lax.axis_index("gr")
    x, z = lax.rem(me, X), lax.div(me, X)
    core, y = lax.rem(mine, CORES), lax.div(mine, CORES)

    def at(dx, dz):
        return lax.rem(z + (dz + z_chips), z_chips) * X + lax.rem(x + (dx + X), X)

    def at_y(dy, c):
        return lax.rem(y + (dy + y_chips), y_chips) * CORES + c

    def rows(origin, first=0):
        return pl.multiple_of(origin * tile + first, CODE)

    loads = [
        pltpu.make_async_copy(src, dst, local_sem.at[i])
        for i, (src, dst) in enumerate(((ip_hbm, ip_ref), (w_hbm, w_ref), (op_hbm, op_ref)))
    ]
    for load in loads:
        load.start()
    barrier = pltpu.get_barrier_semaphore()
    x_peers = [{"gc": at(i, 0)} for i in range(1, X)]
    z_peers = [{"gc": at(0, i)} for i in range(1, z_chips)]
    greeted = x_peers + z_peers + [{"gr": at_y(1, core)}, {"gr": at_y(-1, core)}, {"gr": at_y(0, 1 - core)}]
    for peer in greeted:
        pl.semaphore_signal(barrier, inc=1, device_id=peer, device_id_type=MESH)
    for load in loads:
        load.wait()

    spots = br * bc
    on = [(ip_ref[p // bc, p % bc] > 0).astype(jnp.int32) for p in range(spots)]
    spare = CAP - sum(on)
    count = jnp.int32(0)
    place = [jnp.int32(0)] * CAP
    for p in range(spots):
        filler = jnp.logical_and(on[p] == 0, spare > 0).astype(jnp.int32)
        spare = spare - filler
        used = on[p] + filler
        for s in range(CAP):
            place[s] = place[s] + jnp.where(count == s, used, 0) * p
        count = count + used

    def reach(p):
        return range(max(0, p - (spots - CAP)), min(CAP - 1, p) + 1)

    def block_of(p):
        r, c = p // bc, p % bc
        return w_ref[r * blk : (r + 1) * blk, c * blk : (c + 1) * blk]

    for c in range(bc):
        total = jnp.zeros((1, blk), f32)
        for r in range(br):
            block = block_of(r * bc + c).astype(f32)
            total += jnp.sum(block, axis=0, keepdims=True) * on[r * bc + c].astype(f32)
        x_sums[x, c : c + 1, :] = total
    code_row = lax.broadcasted_iota(jnp.int32, (CODE, blk), 0)
    codes = jnp.zeros((CODE, blk), f32)
    for s in range(CAP):
        slot = jnp.zeros((blk, blk), f32)
        for p in range(s, s + spots - CAP + 1):
            slot += block_of(p).astype(f32) * (jnp.where(place[s] == p, on[p], 0).astype(f32))
        slot = slot.astype(bf16)
        bbuf[pl.ds(rows(me, s * blk), blk), :] = slot
        abuf[pl.ds(rows(mine, s * blk), blk), :] = slot
        codes = jnp.where(code_row == s, place[s].astype(f32), codes)
    codes = codes.astype(bf16)
    bbuf[pl.ds(rows(me, data), CODE), :] = codes
    abuf[pl.ds(rows(mine, data), CODE), :] = codes

    pl.semaphore_wait(barrier, len(greeted))

    def cut(first, size, which):
        low = (size // 2 + CODE - 1) // CODE * CODE
        return (first, low) if which == 0 else (first + low, size - low)

    P_PART, Q_PART = (0, P_ROWS), (P_ROWS, tile - P_ROWS)

    def b_copy(origin, part, dst, recv):
        ref = bbuf.at[pl.ds(rows(origin, part[0]), part[1]), :]
        return pltpu.make_async_remote_copy(
            src_ref=ref, dst_ref=ref, send_sem=send_sem.at[0], recv_sem=recv,
            device_id={"gc": dst}, device_id_type=MESH,
        )

    Q = X

    def z_copy(s, h, item):
        sign = 1 - 2 * s
        part = Q_PART if item == Q else P_PART
        if h == z_half:
            part = cut(*part, s)
        origin = at(0 if item == Q else item, -sign * (h - 1))
        return b_copy(origin, part, at(0, sign), z_recv.at[s, h - 1, item])

    PX = z_chips

    def x_copy(d, k, item):
        sign = 1 - 2 * d
        part = P_PART if item == PX else Q_PART
        if k == x_half:
            part = cut(*part, d)
        origin = at(-sign * (k - 1), 0 if item == PX else item)
        return b_copy(origin, part, at(sign, 0), x_recv.at[d, k - 1, item])

    def a_copy(origin, part, dst, recv):
        ref = abuf.at[pl.ds(rows(origin, part[0]), part[1]), :]
        return pltpu.make_async_remote_copy(
            src_ref=ref, dst_ref=ref, send_sem=send_sem.at[1], recv_sem=recv,
            device_id={"gr": dst}, device_id_type=MESH,
        )

    def y_copy(s, h, piece):
        sign = 1 - 2 * s
        return a_copy(at_y(-sign * (h - 1), core), cut(0, tile, piece), at_y(sign, core), y_recv.at[s, h - 1, piece])

    def sib_copy(dy, c):
        return a_copy(at_y(dy, c), (0, tile), at_y(0, 1 - c), sib_recv.at[dy % y_chips])

    def small(ref, index, peer, k):
        return pltpu.make_async_remote_copy(
            src_ref=ref.at[index], dst_ref=ref.at[index], send_sem=send_sem.at[k], recv_sem=small_recv.at[k - 2],
            device_id=peer, device_id_type=MESH,
        )

    def all_small(ref, n, peer, k):
        view = ref.at[pl.ds(0, n)]
        return pltpu.make_async_remote_copy(
            src_ref=view, dst_ref=view, send_sem=send_sem.at[k], recv_sem=small_recv.at[k - 2],
            device_id=peer, device_id_type=MESH,
        )

    X_SUMS, Z_SUMS, INVERSES, TOTALS = 2, 3, 4, 5

    def y_step(h):
        for piece in range(2):
            for s in range(2):
                if h < y_half or piece == s:
                    y_copy(s, h, piece).wait_recv()
                if h + 1 < y_half or (h < y_half and piece == s):
                    y_copy(s, h + 1, piece).start()
        for dy in (-h, h) if h < y_half else (h,):
            sib_copy(dy, core).start()

    def x_step(k, dz):
        for d in range(2):
            x_copy(d, k, dz).wait_recv()
            if k < x_half:
                x_copy(d, k + 1, dz).start()

    def z_step(h, item):
        for s in range(2):
            z_copy(s, h, item).wait_recv()
            if h < z_half:
                z_copy(s, h + 1, item).start()

    def spread(t, buf, dst, r_base, c_base, inverse=None):
        codes = buf[pl.ds(rows(t, data), CODE), :].astype(f32)
        places = [codes[s : s + 1, :] for s in range(CAP)]
        slots = [buf[pl.ds(rows(t, s * blk), blk), :] for s in range(CAP)]
        if inverse is not None:
            for s in range(CAP):
                factor = sum(
                    inverse[c : c + 1, :] * sum((places[s] == float(r * bc + c)).astype(f32) for r in range(br))
                    for c in range(bc)
                )
                slots[s] = (slots[s].astype(f32) * factor).astype(bf16)
        for p in range(spots):
            block = sum(slots[s] * (places[s] == float(p)).astype(f32).astype(bf16) for s in reach(p))
            r, c = p // bc, p % bc
            dst[pl.ds(r_base + r * blk, blk), pl.ds(c_base + c * blk, blk)] = block

    def left():
        per = X * br // bc

        @pl.loop(0, z_chips)
        def _(zz):
            for i in range(per):
                t = zz * per + i
                spread(t, abuf, adense.at[zz], 0, i * bc * blk, inverses[t])

    def quad(dz, first=False):
        zz = lax.rem(z + (dz + z_chips), z_chips)

        @pl.loop(0, X)
        def _(i):
            spread(zz * X + i, bbuf, bdense.at[zz], pl.multiple_of(i * (br * blk), blk), 0)

        term = jnp.dot(adense[zz], bdense[zz], preferred_element_type=f32)
        acc[...] = term if first else acc[...] + term

    for peer in x_peers:
        small(x_sums, x, peer, X_SUMS).start()
    for s in range(2):
        z_copy(s, 1, Q).start()
        x_copy(s, 1, PX).start()
    for piece in range(2):
        for s in range(2):
            y_copy(s, 1, piece).start()
    for s in range(2):
        z_copy(s, 1, 0).start()
        x_copy(s, 1, 0).start()
    sib_copy(0, core).start()

    all_small(x_sums, X - 1, x_peers[0], X_SUMS).wait_recv()
    z_sums[z] = jnp.sum(x_sums[...], axis=0)
    for peer in z_peers:
        small(z_sums, z, peer, Z_SUMS).start()
    for d in range(2):
        x_copy(d, 1, PX).wait_recv()
        x_copy(d, 2, PX).start()
        for s in range(2):
            z_copy(s, 1, (X - 1) if d == 0 else 1).start()
    for d in range(2):
        x_copy(d, 2, PX).wait_recv()
    for s in range(2):
        z_copy(s, 1, x_half).start()

    for h in range(1, z_half + 1):
        last = h == z_half
        for s in range(2):
            z_copy(s, h, Q).wait_recv()
            if not last:
                z_copy(s, h + 1, Q).start()
                for d in range(2):
                    x_copy(d, 1, (-h if s == 0 else h) % z_chips).start()
        if last:
            for d in range(2):
                x_copy(d, 1, h).start()
        if h == 1:
            x_step(1, 0)
        y_now = {1: (1,), 2: (2, 3)}.get(h, ())
        z_step(h, 0)
        if h == 1:
            all_small(z_sums, z_chips - 1, z_peers[0], Z_SUMS).wait_recv()
            inverses[mine] = 1.0 / jnp.sum(z_sums[...], axis=0)
        for i in y_now[:1]:
            y_step(i)
        if h == 3:
            y_step(4)
            for dy in range(y_chips):
                sib_copy(dy, 1 - core).wait_recv()
            for i in range(1, gr):
                small(inverses, mine, {"gr": lax.rem(mine + i, gr)}, INVERSES).start()
        z_step(h, 1)
        z_step(h, X - 1)
        if last:
            all_small(inverses, gr - 1, {"gr": 0}, INVERSES).wait_recv()
            left()
            x_step(2, 0)
            quad(0, first=True)
        for i in y_now[1:]:
            y_step(i)
        z_step(h, x_half)
        for dz in (h % z_chips, -h % z_chips) if not last else (h,):
            x_step(1, dz)
    for h in range(1, z_half):
        for dz in (h, z_chips - h):
            x_step(2, dz)
            quad(dz)
    x_step(2, z_half)
    quad(z_half)

    for c in range(bc):
        total = jnp.zeros((1, blk), f32)
        for r in range(br):
            block = acc[r * blk : (r + 1) * blk, c * blk : (c + 1) * blk] * op_ref[r, c].astype(f32)
            block = block * block
            acc[r * blk : (r + 1) * blk, c * blk : (c + 1) * blk] = block
            total += jnp.sum(block, axis=0, keepdims=True)
        totals[me, c : c + 1, :] = total
    far_first = sorted(
        ((dx, dz) for dx in range(X) for dz in range(z_chips) if dx or dz),
        key=lambda p: -(min(p[0], X - p[0]) + min(p[1], z_chips - p[1])),
    )
    for dx, dz in far_first:
        small(totals, me, {"gc": at(dx, dz)}, TOTALS).start()
    all_small(totals, gc - 1, {"gc": 0}, TOTALS).wait_recv()
    factor = float(gc * br * blk) / jnp.sum(totals[...], axis=0)
    for c in range(bc):
        o_ref[:, c * blk : (c + 1) * blk] = (acc[:, c * blk : (c + 1) * blk] * factor[c : c + 1, :]).astype(bf16)

    b_copy(0, (0, (gc - 1) * tile), 0, z_recv.at[0, 0, 0]).wait_send()
    a_copy(0, (0, (gr - 1) * tile), 0, y_recv.at[0, 0, 0]).wait_send()
    all_small(x_sums, X - 1, x_peers[0], X_SUMS).wait_send()
    all_small(z_sums, z_chips - 1, z_peers[0], Z_SUMS).wait_send()
    all_small(inverses, gr - 1, {"gr": 0}, INVERSES).wait_send()
    all_small(totals, gc - 1, {"gc": 0}, TOTALS).wait_send()


def solution(mesh):
    gc, gr = mesh.shape["gc"], mesh.shape["gr"]

    def shards(weights, in_pattern, out_pattern):
        rows, cols = weights.shape
        br, bc = in_pattern.shape
        blk = rows // br
        tile = CAP * blk + CODE
        z_chips, y_chips = gc // X, gr // CORES
        dma = pltpu.SemaphoreType.DMA
        bf16, f32 = jnp.bfloat16, jnp.float32
        return pl.pallas_call(
            functools.partial(kernel, gc, gr, blk),
            out_shape=jax.ShapeDtypeStruct(weights.shape, weights.dtype),
            in_specs=[pl.BlockSpec(memory_space=pl.ANY)] * 3,
            out_specs=pl.BlockSpec(memory_space=pltpu.VMEM),
            scratch_shapes=[
                pltpu.VMEM((rows, cols), bf16),
                pltpu.SMEM((br, bc), jnp.int32),
                pltpu.SMEM((br, bc), jnp.int32),
                pltpu.VMEM((gc * tile, blk), bf16),
                pltpu.VMEM((gr * tile, blk), bf16),
                pltpu.VMEM((z_chips, X * rows, cols), bf16),
                pltpu.VMEM((z_chips, rows, X * rows), bf16),
                pltpu.VMEM((rows, cols), f32),
                pltpu.VMEM((X, bc, blk), f32),
                pltpu.VMEM((z_chips, bc, blk), f32),
                pltpu.VMEM((gr, bc, blk), f32),
                pltpu.VMEM((gc, bc, blk), f32),
                dma((2, z_chips // 2, X + 1)),
                dma((2, X // 2, z_chips + 1)),
                dma((2, y_chips // 2, 2)),
                dma((y_chips,)),
                dma((4,)),
                dma((6,)),
                dma((3,)),
            ],
            compiler_params=pltpu.CompilerParams(
                collective_id=0, has_side_effects=True, vmem_limit_bytes=48 << 20
            ),
        )(weights, in_pattern, out_pattern)

    spec = P("gc", "gr")
    return jax.shard_map(shards, mesh=mesh, in_specs=(spec, spec, spec), out_specs=spec, check_vma=False)
```

```python
import functools

import jax
import jax.numpy as jnp
from jax import lax
from jax.experimental import pallas as pl
from jax.experimental.pallas import tpu as pltpu
from jax.sharding import PartitionSpec as P

MESH = pl.DeviceIdType.MESH
X = 4
CORES = 2
CAP = 4
CODE = 16
P_ROWS = 208


def halves(first, size):
    low = (size // 2 + CODE - 1) // CODE * CODE
    return (first, low), (first + low, size - low)


def plan(z_chips, y_chips, tile):
    row, hop, start, take = 5.5e-3, 1.75, 0.08, 0.05
    spread, dot, left = 0.5, 0.4, 0.25
    z_half, x_half, y_half = z_chips // 2, X // 2, y_chips // 2
    Q, PX = X, z_chips
    p_part, q_part = (0, P_ROWS), (P_ROWS, tile - P_ROWS)
    now, serial, free, arrivals, steps, done = 0.0, 0, {}, [], [], set()
    work = []

    def part(kind, way, k, item):
        if kind == "y":
            return halves(0, tile)[item]
        if kind == "z":
            whole = q_part if item == Q else p_part
            return halves(*whole)[way] if k == z_half else whole
        whole = p_part if item == PX else q_part
        return halves(*whole)[way] if k == x_half else whole

    def arrive(when, step):
        nonlocal serial
        serial += 1
        arrivals.append((when, serial, step))

    def send(kind, way, k, item):
        nonlocal now
        now += start
        free[kind, way] = max(now, free.get((kind, way), 0.0)) + part(kind, way, k, item)[1] * row
        arrive(free[kind, way] + hop, (kind, way, k, item))

    def small(kind, far, step):
        arrive(max(now, free.get((kind, 0), 0.0), free.get((kind, 1), 0.0)) + hop + far, step)

    def complete(dz):
        if dz == 0:
            need = {("x", d, k, PX) for d in range(2) for k in (1, 2)}
        else:
            ways = (0, 1) if dz == z_half else (1,) if dz < z_half else (0,)
            need = {("z", s, min(dz, z_chips - dz), item) for s in ways for item in range(X + 1)}
        need |= {("x", d, k, dz) for d in range(2) for k in range(1, x_half + 1)}
        return need <= done

    small("x", 1.0, ("x_sums",))
    for s in range(2):
        send("z", s, 1, Q)
        send("x", s, 1, PX)
    for piece in range(2):
        for s in range(2):
            send("y", s, 1, piece)
    for s in range(2):
        send("z", s, 1, 0)
        send("x", s, 1, 0)
    waiting = [dz for h in range(z_half + 1) for dz in dict.fromkeys((h, -h % z_chips))]
    scaled = False
    while arrivals or work:
        arrivals.sort()
        if not arrivals or (work and arrivals[0][0] > now):
            step = work.pop(0)
            steps.append(step)
            now += {"spread": spread, "dot": dot, "left": left}[step[0]]
            if step[0] == "spread":
                done.add(step)
        else:
            when, _, step = arrivals.pop(0)
            now = max(now, when) + take
            steps.append(step)
            done.add(step)
            kind = step[0]
            if kind == "z":
                _, s, h, item = step
                if h < z_half:
                    send("z", s, h + 1, item)
                if item == Q and (h < z_half or ("z", 1 - s, h, Q) in done):
                    for d in range(2):
                        send("x", d, 1, (h if s else -h) % z_chips)
            elif kind == "x":
                _, d, k, item = step
                if k < x_half:
                    send("x", d, k + 1, item)
                if item == PX and (k < x_half or ("x", 1 - d, k, PX) in done):
                    for s in range(2):
                        send("z", s, 1, (k if d else -k) % X)
            elif kind == "y":
                _, s, h, piece = step
                if h + 1 < y_half or (h < y_half and piece == s):
                    send("y", s, h + 1, piece)
            elif kind == "x_sums":
                small("z", 4.0, ("z_sums",))
            elif kind == "inverses":
                work[:0] = [("left", zz) for zz in range(z_chips)]
                scaled = True
            if ("inverses",) not in done and not any(a[2][0] in ("y", "z_sums", "x_sums", "inverses") for a in arrivals):
                steps.append(("share",))
                small("y", 4.0, ("inverses",))
        for dz in list(waiting):
            if complete(dz):
                waiting.remove(dz)
                work.append(("spread", dz))
        if scaled:
            for dz in range(z_chips):
                if ("spread", dz) in done and ("dot", dz) not in done:
                    done.add(("dot", dz))
                    work.append(("dot", dz))
    return steps, now


def kernel(
    gc, gr, blk,
    w_hbm, ip_hbm, op_hbm, o_ref,
    w_ref, ip_ref, op_ref, bbuf, abuf, bdense, adense, acc, x_sums, z_sums, inverses, totals,
    z_recv, x_recv, y_recv, sib_recv, small_recv, send_sem, local_sem,
):
    br, bc = ip_ref.shape
    z_chips, y_chips = gc // X, gr // CORES
    x_half, y_half, z_half = X // 2, y_chips // 2, z_chips // 2
    data = CAP * blk
    tile = data + CODE
    f32, bf16 = jnp.float32, jnp.bfloat16

    me = lax.axis_index("gc")
    mine = lax.axis_index("gr")
    x, z = lax.rem(me, X), lax.div(me, X)
    core, y = lax.rem(mine, CORES), lax.div(mine, CORES)

    def at(dx, dz):
        return lax.rem(z + (dz + z_chips), z_chips) * X + lax.rem(x + (dx + X), X)

    def at_y(dy, c):
        return lax.rem(y + (dy + y_chips), y_chips) * CORES + c

    def rows(origin, first=0):
        return pl.multiple_of(origin * tile + first, CODE)

    loads = [
        pltpu.make_async_copy(src, dst, local_sem.at[i])
        for i, (src, dst) in enumerate(((ip_hbm, ip_ref), (w_hbm, w_ref), (op_hbm, op_ref)))
    ]
    for load in loads:
        load.start()
    barrier = pltpu.get_barrier_semaphore()
    x_peers = [{"gc": at(i, 0)} for i in range(1, X)]
    z_peers = [{"gc": at(0, i)} for i in range(1, z_chips)]
    greeted = x_peers + z_peers + [{"gr": at_y(1, core)}, {"gr": at_y(-1, core)}, {"gr": at_y(0, 1 - core)}]
    for peer in greeted:
        pl.semaphore_signal(barrier, inc=1, device_id=peer, device_id_type=MESH)
    for load in loads:
        load.wait()

    spots = br * bc
    on = [(ip_ref[p // bc, p % bc] > 0).astype(jnp.int32) for p in range(spots)]
    spare = CAP - sum(on)
    count = jnp.int32(0)
    place = [jnp.int32(0)] * CAP
    for p in range(spots):
        filler = jnp.logical_and(on[p] == 0, spare > 0).astype(jnp.int32)
        spare = spare - filler
        used = on[p] + filler
        for s in range(CAP):
            place[s] = place[s] + jnp.where(count == s, used, 0) * p
        count = count + used

    def reach(p):
        return range(max(0, p - (spots - CAP)), min(CAP - 1, p) + 1)

    def block_of(p):
        r, c = p // bc, p % bc
        return w_ref[r * blk : (r + 1) * blk, c * blk : (c + 1) * blk]

    for c in range(bc):
        total = jnp.zeros((1, blk), f32)
        for r in range(br):
            block = block_of(r * bc + c).astype(f32)
            total += jnp.sum(block, axis=0, keepdims=True) * on[r * bc + c].astype(f32)
        x_sums[x, c : c + 1, :] = total
    code_row = lax.broadcasted_iota(jnp.int32, (CODE, blk), 0)
    codes = jnp.zeros((CODE, blk), f32)
    for s in range(CAP):
        slot = jnp.zeros((blk, blk), f32)
        for p in range(s, s + spots - CAP + 1):
            slot += block_of(p).astype(f32) * (jnp.where(place[s] == p, on[p], 0).astype(f32))
        slot = slot.astype(bf16)
        bbuf[pl.ds(rows(me, s * blk), blk), :] = slot
        abuf[pl.ds(rows(mine, s * blk), blk), :] = slot
        codes = jnp.where(code_row == s, place[s].astype(f32), codes)
    codes = codes.astype(bf16)
    bbuf[pl.ds(rows(me, data), CODE), :] = codes
    abuf[pl.ds(rows(mine, data), CODE), :] = codes

    pl.semaphore_wait(barrier, len(greeted))

    P_PART, Q_PART = (0, P_ROWS), (P_ROWS, tile - P_ROWS)

    def b_copy(origin, part, dst, recv):
        ref = bbuf.at[pl.ds(rows(origin, part[0]), part[1]), :]
        return pltpu.make_async_remote_copy(
            src_ref=ref, dst_ref=ref, send_sem=send_sem.at[0], recv_sem=recv,
            device_id={"gc": dst}, device_id_type=MESH,
        )

    Q = X

    def z_copy(s, h, item):
        sign = 1 - 2 * s
        part = Q_PART if item == Q else P_PART
        if h == z_half:
            part = halves(*part)[s]
        origin = at(0 if item == Q else item, -sign * (h - 1))
        return b_copy(origin, part, at(0, sign), z_recv.at[s, h - 1, item])

    PX = z_chips

    def x_copy(d, k, item):
        sign = 1 - 2 * d
        part = P_PART if item == PX else Q_PART
        if k == x_half:
            part = halves(*part)[d]
        origin = at(-sign * (k - 1), 0 if item == PX else item)
        return b_copy(origin, part, at(sign, 0), x_recv.at[d, k - 1, item])

    def a_copy(origin, part, dst, recv):
        ref = abuf.at[pl.ds(rows(origin, part[0]), part[1]), :]
        return pltpu.make_async_remote_copy(
            src_ref=ref, dst_ref=ref, send_sem=send_sem.at[1], recv_sem=recv,
            device_id={"gr": dst}, device_id_type=MESH,
        )

    def y_copy(s, h, piece):
        sign = 1 - 2 * s
        return a_copy(at_y(-sign * (h - 1), core), halves(0, tile)[piece], at_y(sign, core), y_recv.at[s, h - 1, piece])

    def sib_copy(dy, c):
        return a_copy(at_y(dy, c), (0, tile), at_y(0, 1 - c), sib_recv.at[dy % y_chips])

    def small(ref, index, peer, k):
        return pltpu.make_async_remote_copy(
            src_ref=ref.at[index], dst_ref=ref.at[index], send_sem=send_sem.at[k], recv_sem=small_recv.at[k - 2],
            device_id=peer, device_id_type=MESH,
        )

    def all_small(ref, n, peer, k):
        view = ref.at[pl.ds(0, n)]
        return pltpu.make_async_remote_copy(
            src_ref=view, dst_ref=view, send_sem=send_sem.at[k], recv_sem=small_recv.at[k - 2],
            device_id=peer, device_id_type=MESH,
        )

    X_SUMS, Z_SUMS, INVERSES, TOTALS = 2, 3, 4, 5

    def spread(t, buf, dst, r_base, c_base, inverse=None):
        codes = buf[pl.ds(rows(t, data), CODE), :].astype(f32)
        places = [codes[s : s + 1, :] for s in range(CAP)]
        slots = [buf[pl.ds(rows(t, s * blk), blk), :] for s in range(CAP)]
        if inverse is not None:
            for s in range(CAP):
                factor = sum(
                    inverse[c : c + 1, :] * sum((places[s] == float(r * bc + c)).astype(f32) for r in range(br))
                    for c in range(bc)
                )
                slots[s] = (slots[s].astype(f32) * factor).astype(bf16)
        for p in range(spots):
            block = sum(slots[s] * (places[s] == float(p)).astype(f32).astype(bf16) for s in reach(p))
            r, c = p // bc, p % bc
            dst[pl.ds(r_base + r * blk, blk), pl.ds(c_base + c * blk, blk)] = block

    def z_row(dz):
        return lax.rem(z + (dz + z_chips), z_chips)

    def left(i):
        per = X * br // bc
        for k in range(per):
            t = i * per + k
            spread(t, abuf, adense.at[i], 0, k * bc * blk, inverses[t])

    def right(dz):
        zz = z_row(dz)

        @pl.loop(0, X)
        def _(i):
            spread(zz * X + i, bbuf, bdense.at[zz], pl.multiple_of(i * (br * blk), blk), 0)

    for peer in x_peers:
        small(x_sums, x, peer, X_SUMS).start()
    for s in range(2):
        z_copy(s, 1, Q).start()
        x_copy(s, 1, PX).start()
    for piece in range(2):
        for s in range(2):
            y_copy(s, 1, piece).start()
    for s in range(2):
        z_copy(s, 1, 0).start()
        x_copy(s, 1, 0).start()
    sib_copy(0, core).start()

    taken = set()
    first = True
    for step in plan(z_chips, y_chips, tile)[0]:
        kind = step[0]
        taken.add(step)
        if kind == "z":
            _, s, h, item = step
            z_copy(s, h, item).wait_recv()
            if h < z_half:
                z_copy(s, h + 1, item).start()
            if item == Q and (h < z_half or ("z", 1 - s, h, Q) in taken):
                for d in range(2):
                    x_copy(d, 1, (h if s else -h) % z_chips).start()
        elif kind == "x":
            _, d, k, item = step
            x_copy(d, k, item).wait_recv()
            if k < x_half:
                x_copy(d, k + 1, item).start()
            if item == PX and (k < x_half or ("x", 1 - d, k, PX) in taken):
                for s in range(2):
                    z_copy(s, 1, (k if d else -k) % X).start()
        elif kind == "y":
            _, s, h, piece = step
            y_copy(s, h, piece).wait_recv()
            if h + 1 < y_half or (h < y_half and piece == s):
                y_copy(s, h + 1, piece).start()
            other = ("y", s, h, 1 - piece) if h < y_half else ("y", 1 - s, h, 1 - piece)
            if other in taken:
                sib_copy(h if s or h == y_half else -h, core).start()
        elif kind == "x_sums":
            all_small(x_sums, X - 1, x_peers[0], X_SUMS).wait_recv()
            z_sums[z] = jnp.sum(x_sums[...], axis=0)
            for peer in z_peers:
                small(z_sums, z, peer, Z_SUMS).start()
        elif kind == "z_sums":
            all_small(z_sums, z_chips - 1, z_peers[0], Z_SUMS).wait_recv()
            inverses[mine] = 1.0 / jnp.sum(z_sums[...], axis=0)
        elif kind == "share":
            for dy in range(y_chips):
                sib_copy(dy, 1 - core).wait_recv()
            for i in range(1, gr):
                small(inverses, mine, {"gr": lax.rem(mine + i, gr)}, INVERSES).start()
        elif kind == "inverses":
            all_small(inverses, gr - 1, {"gr": 0}, INVERSES).wait_recv()
        elif kind == "left":
            left(step[1])
        elif kind == "spread":
            right(step[1])
        elif kind == "dot":
            zz = z_row(step[1])
            term = jnp.dot(adense[zz], bdense[zz], preferred_element_type=f32)
            acc[...] = term if first else acc[...] + term
            first = False

    for c in range(bc):
        total = jnp.zeros((1, blk), f32)
        for r in range(br):
            block = acc[r * blk : (r + 1) * blk, c * blk : (c + 1) * blk] * op_ref[r, c].astype(f32)
            block = block * block
            acc[r * blk : (r + 1) * blk, c * blk : (c + 1) * blk] = block
            total += jnp.sum(block, axis=0, keepdims=True)
        totals[me, c : c + 1, :] = total
    far_first = sorted(
        ((dx, dz) for dx in range(X) for dz in range(z_chips) if dx or dz),
        key=lambda p: -(min(p[0], X - p[0]) + min(p[1], z_chips - p[1])),
    )
    for dx, dz in far_first:
        small(totals, me, {"gc": at(dx, dz)}, TOTALS).start()
    all_small(totals, gc - 1, {"gc": 0}, TOTALS).wait_recv()
    factor = float(gc * br * blk) / jnp.sum(totals[...], axis=0)
    for c in range(bc):
        o_ref[:, c * blk : (c + 1) * blk] = (acc[:, c * blk : (c + 1) * blk] * factor[c : c + 1, :]).astype(bf16)

    b_copy(0, (0, (gc - 1) * tile), 0, z_recv.at[0, 0, 0]).wait_send()
    a_copy(0, (0, (gr - 1) * tile), 0, y_recv.at[0, 0, 0]).wait_send()
    all_small(x_sums, X - 1, x_peers[0], X_SUMS).wait_send()
    all_small(z_sums, z_chips - 1, z_peers[0], Z_SUMS).wait_send()
    all_small(inverses, gr - 1, {"gr": 0}, INVERSES).wait_send()
    all_small(totals, gc - 1, {"gc": 0}, TOTALS).wait_send()


def solution(mesh):
    gc, gr = mesh.shape["gc"], mesh.shape["gr"]

    def shards(weights, in_pattern, out_pattern):
        rows, cols = weights.shape
        br, bc = in_pattern.shape
        blk = rows // br
        tile = CAP * blk + CODE
        z_chips, y_chips = gc // X, gr // CORES
        dma = pltpu.SemaphoreType.DMA
        bf16, f32 = jnp.bfloat16, jnp.float32
        return pl.pallas_call(
            functools.partial(kernel, gc, gr, blk),
            out_shape=jax.ShapeDtypeStruct(weights.shape, weights.dtype),
            in_specs=[pl.BlockSpec(memory_space=pl.ANY)] * 3,
            out_specs=pl.BlockSpec(memory_space=pltpu.VMEM),
            scratch_shapes=[
                pltpu.VMEM((rows, cols), bf16),
                pltpu.SMEM((br, bc), jnp.int32),
                pltpu.SMEM((br, bc), jnp.int32),
                pltpu.VMEM((gc * tile, blk), bf16),
                pltpu.VMEM((gr * tile, blk), bf16),
                pltpu.VMEM((z_chips, X * rows, cols), bf16),
                pltpu.VMEM((z_chips, rows, X * rows), bf16),
                pltpu.VMEM((rows, cols), f32),
                pltpu.VMEM((X, bc, blk), f32),
                pltpu.VMEM((z_chips, bc, blk), f32),
                pltpu.VMEM((gr, bc, blk), f32),
                pltpu.VMEM((gc, bc, blk), f32),
                dma((2, z_chips // 2, X + 1)),
                dma((2, X // 2, z_chips + 1)),
                dma((2, y_chips // 2, 2)),
                dma((y_chips,)),
                dma((4,)),
                dma((6,)),
                dma((3,)),
            ],
            compiler_params=pltpu.CompilerParams(
                collective_id=0, has_side_effects=True, vmem_limit_bytes=48 << 20
            ),
        )(weights, in_pattern, out_pattern)

    spec = P("gc", "gr")
    return jax.shard_map(shards, mesh=mesh, in_specs=(spec, spec, spec), out_specs=spec, check_vma=False)
```

```python
import functools

import jax
import jax.numpy as jnp
from jax import lax
from jax.experimental import pallas as pl
from jax.experimental.pallas import tpu as pltpu
from jax.sharding import PartitionSpec as P

MESH = pl.DeviceIdType.MESH
X = 4
CORES = 2
CAP = 4
CODE = 16
P_ROWS = 208
ROW, HOP, START, TAKE = 5.5e-3, 1.75, 0.12, 0.08

FIRST = [("z", s, 1, X - 1) for s in range(2)] + [("x", d, 1, 4 + 1) for d in range(2)] + [("y", s, 1, 0) for s in range(2)]
FIRST += [("z", s, 1, 0) for s in range(2)] + [("x", d, 1, 0) for d in range(2)]


def follow(step, done, z_half, y_half):
    kind, way, k, item = step
    ways = range(2)
    both = (kind, 1 - way, k, item) in done
    last = {"x": X // 2, "y": y_half, "z": z_half}[kind]
    steps = [(kind, way, k + 1, item)] if k < last else []
    if kind == "z" and item == X - 1 and both:
        steps += [("x", d, 1, k) for d in ways]
    if kind == "x" and item == z_half + 1 and both:
        steps += [("z", s, 1, k) for s in ways]
    return steps


def halves(first, size):
    low = (size // 2 + CODE - 1) // CODE * CODE
    return (first, low), (first + low, size - low)


def plan(z_chips, y_chips, tile):
    row, hop, start, take = ROW, HOP, START, TAKE
    spread, dot, left = 0.5, 0.4, 0.25
    z_half, x_half, y_half = z_chips // 2, X // 2, y_chips // 2
    Q, PX = X - 1, z_half + 1
    now, serial, free, arrivals, steps, done = 0.0, 0, {}, [], [], set()
    work = []

    def size(kind, way, k, item):
        if kind == "y":
            return halves(0, tile)[way][1] if k == y_half else tile
        first = item != Q if kind == "z" else item == PX
        rows = P_ROWS if first else tile - P_ROWS
        if k == (z_half if kind == "z" else x_half):
            rows = halves(0, rows)[way][1]
        pair = item == 1 if kind == "z" else 0 < item < z_half
        return rows * (2 if pair else 1)

    def arrive(when, step):
        nonlocal serial
        serial += 1
        arrivals.append((when, serial, step))

    def send(kind, way, k, item):
        nonlocal now
        now += start
        free[kind, way] = max(now, free.get((kind, way), 0.0)) + size(kind, way, k, item) * row
        arrive(free[kind, way] + hop, (kind, way, k, item))

    def small(kind, far, step):
        arrive(max(now, free.get((kind, 0), 0.0), free.get((kind, 1), 0.0)) + hop + far, step)

    def complete(dz):
        h = min(dz, z_chips - dz)
        need = {("x", d, k, h) for d in range(2) for k in (1, 2)}
        if dz == 0:
            need |= {("x", d, k, PX) for d in range(2) for k in (1, 2)}
        else:
            ways = (0, 1) if dz == z_half else (1,) if dz < z_half else (0,)
            need |= {("z", s, h, item) for s in ways for item in range(X)}
        return need <= done

    small("x", 1.0, ("x_sums",))
    for step in FIRST:
        send(*step)
    waiting = [dz for h in range(z_half + 1) for dz in dict.fromkeys((h, -h % z_chips))]
    scaled = False
    while arrivals or work:
        arrivals.sort()
        if not arrivals or (work and arrivals[0][0] > now):
            step = work.pop(0)
            steps.append(step)
            now += {"spread": spread, "dot": dot, "left": left}[step[0]]
            if step[0] == "spread":
                done.add(step)
        else:
            when, _, step = arrivals.pop(0)
            now = max(now, when) + take
            steps.append(step)
            done.add(step)
            kind = step[0]
            if kind in ("x", "y", "z"):
                for following in follow(step, done, z_half, y_half):
                    send(*following)
            elif kind == "x_sums":
                small("z", 4.0, ("z_sums",))
            elif kind == "z_sums":
                small("y", 4.0, ("inverses",))
            if not scaled and not any(a[2][0] in ("y", "z_sums", "x_sums", "inverses") for a in arrivals):
                arrive(now + 2.0, ("all",))
                scaled = True
            if kind == "all":
                work[:0] = [("left", dy) for dy in range(y_chips)]
        for dz in list(waiting):
            if complete(dz):
                waiting.remove(dz)
                work.append(("spread", dz))
        if ("all",) in done:
            for dz in range(z_chips):
                if ("spread", dz) in done and ("dot", dz) not in done:
                    done.add(("dot", dz))
                    work.append(("dot", dz))
    return steps, now


def kernel(
    gc, gr, blk,
    w_hbm, ip_hbm, op_hbm, o_ref,
    w_ref, ip_ref, op_ref, pbuf, qbuf, abuf, bdense, adense, acc, x_sums, z_sums, inverses, totals,
    z_recv, x_recv, y_recv, sib_recv, small_recv, send_sem, local_sem,
):
    br, bc = ip_ref.shape
    z_chips, y_chips = gc // X, gr // CORES
    x_half, y_half, z_half = X // 2, y_chips // 2, z_chips // 2
    data = CAP * blk
    tile = data + CODE
    f32, bf16 = jnp.float32, jnp.bfloat16

    me = lax.axis_index("gc")
    mine = lax.axis_index("gr")
    x, z = lax.rem(me, X), lax.div(me, X)
    core, y = lax.rem(mine, CORES), lax.div(mine, CORES)

    def at(dx, dz):
        return lax.rem(z + (dz + z_chips), z_chips) * X + lax.rem(x + (dx + X), X)

    def at_y(dy, c):
        return lax.rem(y + (dy + y_chips), y_chips) * CORES + c

    def slot_of(d, n):
        d %= n
        return 2 * d - 1 if 0 < d <= n // 2 else 2 * (n - d) if d else 0

    loads = [
        pltpu.make_async_copy(src, dst, local_sem.at[i])
        for i, (src, dst) in enumerate(((ip_hbm, ip_ref), (w_hbm, w_ref), (op_hbm, op_ref)))
    ]
    for load in loads:
        load.start()
    barrier = pltpu.get_barrier_semaphore()
    x_peers = [{"gc": at(i, 0)} for i in range(1, X)]
    z_peers = [{"gc": at(0, i)} for i in range(1, z_chips)]
    y_peers = [{"gr": at_y(i, core)} for i in range(1, y_chips)]
    other_core = {"gr": at_y(0, 1 - core)}
    greeted = x_peers + z_peers + y_peers + [other_core]
    for peer in greeted:
        pl.semaphore_signal(barrier, inc=1, device_id=peer, device_id_type=MESH)
    for load in loads:
        load.wait()

    spots = br * bc
    on = [(ip_ref[p // bc, p % bc] > 0).astype(jnp.int32) for p in range(spots)]
    spare = CAP - sum(on)
    count = jnp.int32(0)
    place = [jnp.int32(0)] * CAP
    for p in range(spots):
        filler = jnp.logical_and(on[p] == 0, spare > 0).astype(jnp.int32)
        spare = spare - filler
        used = on[p] + filler
        for s in range(CAP):
            place[s] = place[s] + jnp.where(count == s, used, 0) * p
        count = count + used

    def reach(p):
        return range(max(0, p - (spots - CAP)), min(CAP - 1, p) + 1)

    def block_of(p):
        r, c = p // bc, p % bc
        return w_ref[r * blk : (r + 1) * blk, c * blk : (c + 1) * blk]

    for c in range(bc):
        total = jnp.zeros((1, blk), f32)
        for r in range(br):
            block = block_of(r * bc + c).astype(f32)
            total += jnp.sum(block, axis=0, keepdims=True) * on[r * bc + c].astype(f32)
        x_sums[0, c : c + 1, :] = total
    def put(first, block):
        size = block.shape[0]
        abuf[0, first : first + size, :] = block
        cut = min(max(P_ROWS - first, 0), size)
        if cut > 0:
            pbuf[0, first : first + cut, :] = block[:cut]
        if cut < size:
            qbuf[0, first + cut - P_ROWS : first + size - P_ROWS, :] = block[cut:]

    code_row = lax.broadcasted_iota(jnp.int32, (CODE, blk), 0)
    codes = jnp.zeros((CODE, blk), f32)
    for s in range(CAP):
        slot = sum(
            block_of(p) * jnp.full((1, blk), jnp.where(place[s] == p, on[p], 0).astype(f32)).astype(bf16)
            for p in range(s, s + spots - CAP + 1)
        )
        put(s * blk, slot)
        codes = jnp.where(code_row == s, place[s].astype(f32), codes)
    put(data, codes.astype(bf16))

    pl.semaphore_wait(barrier, len(greeted))

    down = {"z": [{"gc": at(0, 1)}, {"gc": at(0, -1)}], "x": [{"gc": at(1, 0)}, {"gc": at(-1, 0)}],
            "y": [{"gr": at_y(1, core)}, {"gr": at_y(-1, core)}]}
    landed = {"z": z_recv, "x": x_recv, "y": y_recv}
    sent = {"p": send_sem.at[0], "q": send_sem.at[7], "a": send_sem.at[1]}
    which = {"p": pbuf, "q": qbuf, "a": abuf}

    def move(name, src, dst, count, rows, sem, peer):
        ref, (first, size) = which[name], rows
        return pltpu.make_async_remote_copy(
            src_ref=ref.at[src : src + count, first : first + size, :],
            dst_ref=ref.at[dst : dst + count, first : first + size, :],
            send_sem=sent[name], recv_sem=sem, device_id=peer, device_id_type=MESH,
        )

    def link(kind, way, k, item):
        sign = 1 - 2 * way
        n = {"z": z_chips, "x": X, "y": y_chips}[kind]
        here, there = slot_of(-sign * (k - 1), n), slot_of(-sign * k, n)
        whole = {"p": (0, P_ROWS), "q": (0, tile - P_ROWS), "a": (0, tile)}
        count = 1
        if kind == "y":
            name, src, dst = "a", here, there
        elif (kind == "z") == (item == (X - 1 if kind == "z" else z_half + 1)):
            name = "q"
            if kind == "z":
                src, dst = here, there
            else:
                z0 = 2 * item - 1 if item else 0
                count = 2 if 0 < item < z_half else 1
                src, dst = here * z_chips + z0, there * z_chips + z0
        else:
            name = "p"
            if kind == "x":
                src, dst = here, there
            else:
                x0 = 2 * item - 1 if item else 0
                count = 2 if item == 1 else 1
                src, dst = here * X + x0, there * X + x0
        rows = halves(*whole[name])[way] if k == n // 2 else whole[name]
        sem = landed[kind].at[way, k - 1] if kind == "y" else landed[kind].at[way, k - 1, item]
        return move(name, src, dst, count, rows, sem, down[kind][way])

    def sib_copy(dy):
        i = slot_of(dy, y_chips)
        return move("a", i, y_chips + i, 1, (0, tile), sib_recv.at[i], other_core)

    def small(ref, index, peer, k):
        return pltpu.make_async_remote_copy(
            src_ref=ref.at[0], dst_ref=ref.at[index], send_sem=send_sem.at[k], recv_sem=small_recv.at[k - 2],
            device_id=peer, device_id_type=MESH,
        )

    def all_small(ref, n, peer, k):
        view = ref.at[pl.ds(0, n)]
        return pltpu.make_async_remote_copy(
            src_ref=view, dst_ref=view, send_sem=send_sem.at[k], recv_sem=small_recv.at[k - 2],
            device_id=peer, device_id_type=MESH,
        )

    X_SUMS, Z_SUMS, INVERSES, TOTALS, PASSED = 2, 3, 4, 5, 6

    def pass_on():
        return pltpu.make_async_remote_copy(
            src_ref=inverses.at[pl.ds(0, y_chips)], dst_ref=inverses.at[pl.ds(y_chips, y_chips)],
            send_sem=send_sem.at[PASSED], recv_sem=small_recv.at[PASSED - 2],
            device_id=other_core, device_id_type=MESH,
        )

    def spread(load, dst, r_base, c_base, inverse=None):
        codes = load(data, CODE).astype(f32)
        places = [codes[s : s + 1, :] for s in range(CAP)]
        slots = [load(s * blk, blk) for s in range(CAP)]
        if inverse is not None:
            for s in range(CAP):
                factor = sum(
                    inverse[c : c + 1, :] * sum((places[s] == float(r * bc + c)).astype(f32) for r in range(br))
                    for c in range(bc)
                )
                slots[s] = (slots[s].astype(f32) * factor).astype(bf16)
        for p in range(spots):
            block = sum(slots[s] * (places[s] == float(p)).astype(f32).astype(bf16) for s in reach(p))
            r, c = p // bc, p % bc
            dst[pl.ds(r_base + r * blk, blk), pl.ds(c_base + c * blk, blk)] = block

    def left(dy):
        zz = lax.rem(y + dy, y_chips)
        for other in range(CORES):
            i = other * y_chips + slot_of(dy, y_chips)
            c_base = pl.multiple_of((core if other == 0 else 1 - core) * (bc * blk), blk)
            spread(lambda first, size, i=i: abuf[i, first : first + size, :], adense.at[zz], 0, c_base, inverses[i])

    def right(dz):
        zs = slot_of(dz, z_chips)

        @pl.loop(0, X)
        def _(i):
            def load(first, size):
                cut = min(max(P_ROWS - first, 0), size)
                parts = []
                if cut > 0:
                    parts.append(pbuf[zs * X + i, first : first + cut, :])
                if cut < size:
                    parts.append(qbuf[i * z_chips + zs, first + cut - P_ROWS : first + size - P_ROWS, :])
                return parts[0] if len(parts) == 1 else jnp.concatenate(parts, axis=0)

            dx = i + jnp.where(i == 2, 1, 0) - jnp.where(i == 3, 1, 0)
            spread(load, bdense.at[zs], pl.multiple_of(lax.rem(x + dx, X) * (br * blk), blk), 0)

    for i, peer in enumerate(x_peers):
        small(x_sums, X - 1 - i, peer, X_SUMS).start()
    for step in FIRST:
        link(*step).start()
    sib_copy(0).start()

    taken = set()
    first = True
    for step in plan(z_chips, y_chips, tile)[0]:
        kind = step[0]
        if kind in landed:
            link(*step).wait_recv()
            for following in follow(step, taken, z_half, y_half):
                link(*following).start()
            if kind == "y" and (step[2] < y_half or ("y", 1 - step[1], y_half, 0) in taken):
                sib_copy(step[2] if step[1] else -step[2]).start()
        elif kind == "x_sums":
            all_small(x_sums, X - 1, x_peers[0], X_SUMS).wait_recv()
            z_sums[0] = jnp.sum(x_sums[...], axis=0)
            for i, peer in enumerate(z_peers):
                small(z_sums, z_chips - 1 - i, peer, Z_SUMS).start()
        elif kind == "z_sums":
            all_small(z_sums, z_chips - 1, z_peers[0], Z_SUMS).wait_recv()
            inverses[0] = 1.0 / jnp.sum(z_sums[...], axis=0)
            for i, peer in enumerate(y_peers):
                small(inverses, slot_of(-1 - i, y_chips), peer, INVERSES).start()
        elif kind == "inverses":
            all_small(inverses, y_chips - 1, y_peers[0], INVERSES).wait_recv()
            pass_on().start()
        elif kind == "all":
            for dy in range(y_chips):
                sib_copy(dy).wait_recv()
            pass_on().wait_recv()
        elif kind == "left":
            left(step[1])
        elif kind == "spread":
            right(step[1])
        elif kind == "dot":
            zz = lax.rem(z + step[1], z_chips)
            term = jnp.dot(adense[zz], bdense[slot_of(step[1], z_chips)], preferred_element_type=f32)
            acc[...] = term if first else acc[...] + term
            first = False
        taken.add(step)

    for c in range(bc):
        total = jnp.zeros((1, blk), f32)
        for r in range(br):
            block = acc[r * blk : (r + 1) * blk, c * blk : (c + 1) * blk] * op_ref[r, c].astype(f32)
            block = block * block
            acc[r * blk : (r + 1) * blk, c * blk : (c + 1) * blk] = block
            total += jnp.sum(block, axis=0, keepdims=True)
        totals[0, c : c + 1, :] = total
    far_first = sorted(
        ((dx, dz) for dx in range(X) for dz in range(z_chips) if dx or dz),
        key=lambda p: -(min(p[0], X - p[0]) + min(p[1], z_chips - p[1])),
    )
    for dx, dz in far_first:
        small(totals, -dz % z_chips * X + -dx % X, {"gc": at(dx, dz)}, TOTALS).start()
    all_small(totals, gc - 1, {"gc": 0}, TOTALS).wait_recv()
    factor = float(gc * br * blk) / jnp.sum(totals[...], axis=0)
    for c in range(bc):
        o_ref[:, c * blk : (c + 1) * blk] = (acc[:, c * blk : (c + 1) * blk] * factor[c : c + 1, :]).astype(bf16)

    neighbour = down["x"][0]
    move("p", 0, 0, gc - 1, (0, P_ROWS), x_recv.at[0, 0, 0], neighbour).wait_send()
    move("q", 0, 0, gc - 1, (0, tile - P_ROWS), x_recv.at[0, 0, 0], neighbour).wait_send()
    move("a", 0, 0, gr - 1, (0, tile), sib_recv.at[0], other_core).wait_send()
    all_small(x_sums, X - 1, x_peers[0], X_SUMS).wait_send()
    all_small(z_sums, z_chips - 1, z_peers[0], Z_SUMS).wait_send()
    all_small(inverses, y_chips - 1, y_peers[0], INVERSES).wait_send()
    pass_on().wait_send()
    all_small(totals, gc - 1, {"gc": 0}, TOTALS).wait_send()


def solution(mesh):
    gc, gr = mesh.shape["gc"], mesh.shape["gr"]

    def shards(weights, in_pattern, out_pattern):
        rows, cols = weights.shape
        br, bc = in_pattern.shape
        blk = rows // br
        tile = CAP * blk + CODE
        z_chips, y_chips = gc // X, gr // CORES
        dma = pltpu.SemaphoreType.DMA
        bf16, f32 = jnp.bfloat16, jnp.float32
        return pl.pallas_call(
            functools.partial(kernel, gc, gr, blk),
            out_shape=jax.ShapeDtypeStruct(weights.shape, weights.dtype),
            in_specs=[pl.BlockSpec(memory_space=pl.ANY)] * 3,
            out_specs=pl.BlockSpec(memory_space=pltpu.VMEM),
            scratch_shapes=[
                pltpu.VMEM((rows, cols), bf16),
                pltpu.SMEM((br, bc), jnp.int32),
                pltpu.SMEM((br, bc), jnp.int32),
                pltpu.VMEM((gc, P_ROWS, blk), bf16),
                pltpu.VMEM((gc, tile - P_ROWS, blk), bf16),
                pltpu.VMEM((gr, tile, blk), bf16),
                pltpu.VMEM((z_chips, X * rows, cols), bf16),
                pltpu.VMEM((z_chips, rows, X * rows), bf16),
                pltpu.VMEM((rows, cols), f32),
                pltpu.VMEM((X, bc, blk), f32),
                pltpu.VMEM((z_chips, bc, blk), f32),
                pltpu.VMEM((gr, bc, blk), f32),
                pltpu.VMEM((gc, bc, blk), f32),
                dma((2, z_chips // 2, X)),
                dma((2, X // 2, z_chips // 2 + 2)),
                dma((2, y_chips // 2)),
                dma((y_chips,)),
                dma((5,)),
                dma((8,)),
                dma((3,)),
            ],
            compiler_params=pltpu.CompilerParams(
                collective_id=0, has_side_effects=True, vmem_limit_bytes=48 << 20
            ),
        )(weights, in_pattern, out_pattern)

    spec = P("gc", "gr")
    return jax.shard_map(shards, mesh=mesh, in_specs=(spec, spec, spec), out_specs=spec, check_vma=False)
```

```python
import functools

import jax
import jax.numpy as jnp
from jax import lax
from jax.experimental import pallas as pl
from jax.experimental.pallas import tpu as pltpu
from jax.sharding import PartitionSpec as P

MESH = pl.DeviceIdType.MESH
X = 4
CORES = 2
CAP = 4
CODE = 16
P_ROWS = 192
ROW, HOP, START, TAKE = 5.5e-3, 2.4, 0.08, 0.05

ALL = 2
RELAYS = 3
P_PIECES, Q_PIECES, Y_PIECES = (ALL,), (0, 1), (0, 1)


def slot_of(d, n):
    d %= n
    return 2 * d - 1 if 0 < d <= n // 2 else 2 * (n - d) if d else 0


def pieces(kind, item, z_chips):
    if kind == "y":
        return Y_PIECES
    return Q_PIECES if (kind == "z") == (item == (X if kind == "z" else z_chips)) else P_PIECES


def ring(kind, z_chips, y_chips):
    return {"x": X, "y": y_chips, "z": z_chips}[kind]


def goes(way, k, piece, n):
    return k < n // 2 or piece in (ALL, way)


def first_copies(z_chips):
    ways = range(2)
    order = (("z", X), ("x", z_chips), ("y", 0), ("z", 0), ("x", 0))
    return [(kind, way, 1, item, piece) for kind, item in order for piece in pieces(kind, item, z_chips) for way in ways]


def follow(step, done, z_chips, y_chips):
    kind, way, k, item, piece = step
    ways = range(2)
    n = ring(kind, z_chips, y_chips)
    steps = [(kind, way, k + 1, item, piece)] if k < n // 2 and goes(way, k + 1, piece, n) else []
    whole = k < n // 2 or piece != ALL or (kind, 1 - way, k, item, piece) in done
    came = slot_of(k if way else -k, n)
    if kind == "z" and item == X and whole:
        steps += [("x", d, 1, came, piece) for d in ways]
    if kind == "x" and item == z_chips and whole:
        steps += [("z", s, 1, came, piece) for s in ways]
    return steps


def halves(first, size):
    low = (size // 2 + CODE - 1) // CODE * CODE
    return (first, low), (first + low, size - low)


def plan(z_chips, y_chips, tile):
    row, hop, start, take = ROW, HOP, START, TAKE
    spread, dot, left = 0.5, 0.4, 0.25
    z_half, x_half, y_half = z_chips // 2, X // 2, y_chips // 2
    Q, PX = X, z_chips
    now, serial, free, arrivals, steps, done = 0.0, 0, {}, [], [], set()
    work = []

    def size(kind, way, k, item, piece):
        first = item != Q if kind == "z" else item == PX
        rows = tile if kind == "y" else P_ROWS if first else tile - P_ROWS
        if piece != ALL:
            return halves(0, rows)[piece][1]
        return halves(0, rows)[way][1] if k == ring(kind, z_chips, y_chips) // 2 else rows

    def arrive(when, step):
        nonlocal serial
        serial += 1
        arrivals.append((when, serial, step))

    def send(*step):
        nonlocal now
        now += start
        free[step[:2]] = max(now, free.get(step[:2], 0.0)) + size(*step) * row
        arrive(free[step[:2]] + hop, step)

    def small(kind, far, step):
        arrive(max(now, free.get((kind, 0), 0.0), free.get((kind, 1), 0.0)) + hop + far, step)

    def complete(dz):
        h = min(dz, z_chips - dz)
        parts = [("x", d, k, slot_of(dz, z_chips)) for d in range(2) for k in (1, 2)]
        if dz == 0:
            parts += [("x", d, k, PX) for d in range(2) for k in (1, 2)]
        else:
            ways = (0, 1) if dz == z_half else (1,) if dz < z_half else (0,)
            parts += [("z", s, h, item) for s in ways for item in range(X + 1)]
        need = {
            (kind, way, k, item, piece)
            for kind, way, k, item in parts
            for piece in pieces(kind, item, z_chips)
            if goes(way, k, piece, ring(kind, z_chips, y_chips))
        }
        return need <= done

    arrive(2.2, ("ready", 0))
    for step in first_copies(z_chips):
        send(*step)
    waiting = [dz for h in range(z_half + 1) for dz in dict.fromkeys((h, -h % z_chips))]
    scaled = False
    while arrivals or work:
        arrivals.sort()
        if not arrivals or (work and arrivals[0][0] > now):
            step = work.pop(0)
            steps.append(step)
            now += {"spread": spread, "dot": dot, "left": left}[step[0]]
            if step[0] == "spread":
                done.add(step)
        else:
            when, _, step = arrivals.pop(0)
            now = max(now, when) + take
            steps.append(step)
            done.add(step)
            kind = step[0]
            if kind in ("x", "y", "z"):
                for following in follow(step, done, z_chips, y_chips):
                    send(*following)
            elif kind == "ready":
                if step[1] + 1 < RELAYS:
                    arrive(now + 2.2, ("ready", step[1] + 1))
                if step[1] == 0:
                    small("x", 1.0, ("x_sums",))
            elif kind == "z_sums":
                small("y", 4.0, ("inverses",))
            if step in (("x_sums",), ("ready", RELAYS - 1)) and {("x_sums",), ("ready", RELAYS - 1)} <= done:
                steps.append(("column",))
                small("z", 4.0, ("z_sums",))
            if not scaled and not any(a[2][0] in ("y", "z_sums", "x_sums", "ready", "inverses") for a in arrivals):
                arrive(now + 2.0, ("all",))
                scaled = True
            if kind == "all":
                work[:0] = [("left", dy) for dy in range(y_chips)]
        for dz in list(waiting):
            if complete(dz):
                waiting.remove(dz)
                work.append(("spread", dz))
        if ("all",) in done:
            for dz in range(z_chips):
                if ("spread", dz) in done and ("dot", dz) not in done:
                    done.add(("dot", dz))
                    work.append(("dot", dz))
    return steps, now


def kernel(
    gc, gr, blk,
    w_hbm, ip_hbm, op_hbm, o_ref,
    w_ref, ip_ref, op_ref, pbuf, qbuf, abuf, bdense, adense, acc, x_sums, z_sums, inverses, totals,
    z_recv, x_recv, y_recv, sib_recv, small_recv, send_sem, local_sem, ready_sem,
):
    br, bc = ip_ref.shape
    z_chips, y_chips = gc // X, gr // CORES
    x_half, y_half, z_half = X // 2, y_chips // 2, z_chips // 2
    data = CAP * blk
    tile = data + CODE
    f32, bf16 = jnp.float32, jnp.bfloat16

    me = lax.axis_index("gc")
    mine = lax.axis_index("gr")
    x, z = lax.rem(me, X), lax.div(me, X)
    core, y = lax.rem(mine, CORES), lax.div(mine, CORES)

    def at(dx, dz):
        return lax.rem(z + (dz + z_chips), z_chips) * X + lax.rem(x + (dx + X), X)

    def at_y(dy, c):
        return lax.rem(y + (dy + y_chips), y_chips) * CORES + c

    loads = [
        pltpu.make_async_copy(src, dst, local_sem.at[i])
        for i, (src, dst) in enumerate(((ip_hbm, ip_ref), (w_hbm, w_ref), (op_hbm, op_ref)))
    ]
    for load in loads:
        load.start()
    barrier = pltpu.get_barrier_semaphore()
    x_peers = [{"gc": at(i, 0)} for i in range(1, X)]
    z_peers = [{"gc": at(0, i)} for i in range(1, z_chips)]
    y_peers = [{"gr": at_y(i, core)} for i in range(1, y_chips)]
    other_core = {"gr": at_y(0, 1 - core)}
    nearest = [{"gc": at(1, 0)}, {"gc": at(-1, 0)}, {"gc": at(0, 1)}, {"gc": at(0, -1)}, {"gr": at_y(1, core)}, {"gr": at_y(-1, core)}]
    greeted = nearest + [other_core]
    for peer in greeted:
        pl.semaphore_signal(barrier, inc=1, device_id=peer, device_id_type=MESH)
    for load in loads:
        load.wait()

    spots = br * bc
    on = [(ip_ref[p // bc, p % bc] > 0).astype(jnp.int32) for p in range(spots)]
    spare = CAP - sum(on)
    count = jnp.int32(0)
    place = [jnp.int32(0)] * CAP
    for p in range(spots):
        filler = jnp.logical_and(on[p] == 0, spare > 0).astype(jnp.int32)
        spare = spare - filler
        used = on[p] + filler
        for s in range(CAP):
            place[s] = place[s] + jnp.where(count == s, used, 0) * p
        count = count + used

    def reach(p):
        return range(max(0, p - (spots - CAP)), min(CAP - 1, p) + 1)

    def block_of(p):
        r, c = p // bc, p % bc
        return w_ref[r * blk : (r + 1) * blk, c * blk : (c + 1) * blk]

    for c in range(bc):
        total = jnp.zeros((1, blk), f32)
        for r in range(br):
            block = block_of(r * bc + c).astype(f32)
            total += jnp.sum(block, axis=0, keepdims=True) * on[r * bc + c].astype(f32)
        x_sums[0, c : c + 1, :] = total
    def put(first, block):
        size = block.shape[0]
        abuf[0, first : first + size, :] = block
        cut = min(max(P_ROWS - first, 0), size)
        if cut > 0:
            pbuf[0, first : first + cut, :] = block[:cut]
        if cut < size:
            qbuf[0, first + cut - P_ROWS : first + size - P_ROWS, :] = block[cut:]

    code_row = lax.broadcasted_iota(jnp.int32, (CODE, blk), 0)
    codes = jnp.zeros((CODE, blk), f32)
    for s in range(CAP):
        slot = sum(
            block_of(p) * jnp.full((1, blk), jnp.where(place[s] == p, on[p], 0).astype(f32)).astype(bf16)
            for p in range(s, s + spots - CAP + 1)
        )
        put(s * blk, slot)
        codes = jnp.where(code_row == s, place[s].astype(f32), codes)
    put(data, codes.astype(bf16))

    pl.semaphore_wait(barrier, len(greeted))

    down = {"z": [{"gc": at(0, 1)}, {"gc": at(0, -1)}], "x": [{"gc": at(1, 0)}, {"gc": at(-1, 0)}],
            "y": [{"gr": at_y(1, core)}, {"gr": at_y(-1, core)}]}
    landed = {"z": z_recv, "x": x_recv, "y": y_recv}
    sent = {"p": send_sem.at[0], "q": send_sem.at[7], "a": send_sem.at[1]}
    which = {"p": pbuf, "q": qbuf, "a": abuf}

    def move(name, src, dst, count, rows, sem, peer):
        ref, (first, size) = which[name], rows
        return pltpu.make_async_remote_copy(
            src_ref=ref.at[src : src + count, first : first + size, :],
            dst_ref=ref.at[dst : dst + count, first : first + size, :],
            send_sem=sent[name], recv_sem=sem, device_id=peer, device_id_type=MESH,
        )

    def link(kind, way, k, item, piece):
        sign = 1 - 2 * way
        n = ring(kind, z_chips, y_chips)
        here, there = slot_of(-sign * (k - 1), n), slot_of(-sign * k, n)
        whole = {"p": (0, P_ROWS), "q": (0, tile - P_ROWS), "a": (0, tile)}
        if kind == "y":
            name, src, dst = "a", here, there
        elif kind == "z":
            name = "q" if item == X else "p"
            src, dst = (here, there) if item == X else (here * X + item, there * X + item)
        else:
            name = "p" if item == z_chips else "q"
            src, dst = (here, there) if item == z_chips else (here * z_chips + item, there * z_chips + item)
        rows = whole[name]
        if piece != ALL or k == n // 2:
            rows = halves(*rows)[way if piece == ALL else piece]
        sem = landed[kind].at[way, k - 1, 2 * item + piece % 2]
        return move(name, src, dst, 1, rows, sem, down[kind][way])

    def sib_copy(dy):
        i = slot_of(dy, y_chips)
        return move("a", i, y_chips + i, 1, (0, tile), sib_recv.at[i], other_core)

    def small(ref, index, peer, k):
        return pltpu.make_async_remote_copy(
            src_ref=ref.at[0], dst_ref=ref.at[index], send_sem=send_sem.at[k], recv_sem=small_recv.at[k - 2],
            device_id=peer, device_id_type=MESH,
        )

    def all_small(ref, n, peer, k):
        view = ref.at[pl.ds(0, n)]
        return pltpu.make_async_remote_copy(
            src_ref=view, dst_ref=view, send_sem=send_sem.at[k], recv_sem=small_recv.at[k - 2],
            device_id=peer, device_id_type=MESH,
        )

    X_SUMS, Z_SUMS, INVERSES, TOTALS, PASSED = 2, 3, 4, 5, 6

    def pass_on():
        return pltpu.make_async_remote_copy(
            src_ref=inverses.at[pl.ds(0, y_chips)], dst_ref=inverses.at[pl.ds(y_chips, y_chips)],
            send_sem=send_sem.at[PASSED], recv_sem=small_recv.at[PASSED - 2],
            device_id=other_core, device_id_type=MESH,
        )

    def spread(load, dst, r_base, c_base, inverse=None):
        codes = load(data, CODE).astype(f32)
        places = [codes[s : s + 1, :] for s in range(CAP)]
        slots = [load(s * blk, blk) for s in range(CAP)]
        if inverse is not None:
            for s in range(CAP):
                factor = sum(
                    inverse[c : c + 1, :] * sum((places[s] == float(r * bc + c)).astype(f32) for r in range(br))
                    for c in range(bc)
                )
                slots[s] = (slots[s].astype(f32) * factor).astype(bf16)
        for p in range(spots):
            block = sum(slots[s] * (places[s] == float(p)).astype(f32).astype(bf16) for s in reach(p))
            r, c = p // bc, p % bc
            dst[pl.ds(r_base + r * blk, blk), pl.ds(c_base + c * blk, blk)] = block

    def left(dy):
        zz = lax.rem(y + dy, y_chips)
        for other in range(CORES):
            i = other * y_chips + slot_of(dy, y_chips)
            c_base = pl.multiple_of((core if other == 0 else 1 - core) * (bc * blk), blk)
            spread(lambda first, size, i=i: abuf[i, first : first + size, :], adense.at[zz], 0, c_base, inverses[i])

    def right(dz):
        zs = slot_of(dz, z_chips)

        @pl.loop(0, X)
        def _(i):
            def load(first, size):
                cut = min(max(P_ROWS - first, 0), size)
                parts = []
                if cut > 0:
                    parts.append(pbuf[zs * X + i, first : first + cut, :])
                if cut < size:
                    parts.append(qbuf[i * z_chips + zs, first + cut - P_ROWS : first + size - P_ROWS, :])
                return parts[0] if len(parts) == 1 else jnp.concatenate(parts, axis=0)

            dx = i + jnp.where(i == 2, 1, 0) - jnp.where(i == 3, 1, 0)
            spread(load, bdense.at[zs], pl.multiple_of(lax.rem(x + dx, X) * (br * blk), blk), 0)

    def relay(i):
        for peer in nearest:
            pl.semaphore_signal(ready_sem.at[i], inc=1, device_id=peer, device_id_type=MESH)

    relay(0)
    for step in first_copies(z_chips):
        link(*step).start()
    sib_copy(0).start()

    taken = set()
    first = True
    for step in plan(z_chips, y_chips, tile)[0]:
        kind = step[0]
        if kind in landed:
            link(*step).wait_recv()
            for following in follow(step, taken, z_chips, y_chips):
                link(*following).start()
            if kind == "y":
                _, way, k, _, piece = step
                if ("y", way if k < y_half else 1 - way, k, 0, 1 - piece) in taken:
                    sib_copy(k if way else -k).start()
        elif kind == "ready":
            pl.semaphore_wait(ready_sem.at[step[1]], len(nearest))
            if step[1] + 1 < RELAYS:
                relay(step[1] + 1)
            if step[1] == 0:
                for i, peer in enumerate(x_peers):
                    small(x_sums, X - 1 - i, peer, X_SUMS).start()
        elif kind == "x_sums":
            all_small(x_sums, X - 1, x_peers[0], X_SUMS).wait_recv()
            z_sums[0] = jnp.sum(x_sums[...], axis=0)
        elif kind == "column":
            for i, peer in enumerate(z_peers):
                small(z_sums, z_chips - 1 - i, peer, Z_SUMS).start()
        elif kind == "z_sums":
            all_small(z_sums, z_chips - 1, z_peers[0], Z_SUMS).wait_recv()
            inverses[0] = 1.0 / jnp.sum(z_sums[...], axis=0)
            for i, peer in enumerate(y_peers):
                small(inverses, slot_of(-1 - i, y_chips), peer, INVERSES).start()
        elif kind == "inverses":
            all_small(inverses, y_chips - 1, y_peers[0], INVERSES).wait_recv()
            pass_on().start()
        elif kind == "all":
            for dy in range(y_chips):
                sib_copy(dy).wait_recv()
            pass_on().wait_recv()
        elif kind == "left":
            left(step[1])
        elif kind == "spread":
            right(step[1])
        elif kind == "dot":
            zz = lax.rem(z + step[1], z_chips)
            term = jnp.dot(adense[zz], bdense[slot_of(step[1], z_chips)], preferred_element_type=f32)
            acc[...] = term if first else acc[...] + term
            first = False
        taken.add(step)

    for c in range(bc):
        total = jnp.zeros((1, blk), f32)
        for r in range(br):
            block = acc[r * blk : (r + 1) * blk, c * blk : (c + 1) * blk] * op_ref[r, c].astype(f32)
            block = block * block
            acc[r * blk : (r + 1) * blk, c * blk : (c + 1) * blk] = block
            total += jnp.sum(block, axis=0, keepdims=True)
        totals[0, c : c + 1, :] = total
    far_first = sorted(
        ((dx, dz) for dx in range(X) for dz in range(z_chips) if dx or dz),
        key=lambda p: -(min(p[0], X - p[0]) + min(p[1], z_chips - p[1])),
    )
    for dx, dz in far_first:
        small(totals, -dz % z_chips * X + -dx % X, {"gc": at(dx, dz)}, TOTALS).start()
    all_small(totals, gc - 1, {"gc": 0}, TOTALS).wait_recv()
    factor = float(gc * br * blk) / jnp.sum(totals[...], axis=0)
    for c in range(bc):
        o_ref[:, c * blk : (c + 1) * blk] = (acc[:, c * blk : (c + 1) * blk] * factor[c : c + 1, :]).astype(bf16)

    neighbour = down["x"][0]
    move("p", 0, 0, gc - 1, (0, P_ROWS), x_recv.at[0, 0, 0], neighbour).wait_send()
    move("q", 0, 0, gc - 1, (0, tile - P_ROWS), x_recv.at[0, 0, 0], neighbour).wait_send()
    move("a", 0, 0, gr - 1, (0, tile), sib_recv.at[0], other_core).wait_send()
    all_small(x_sums, X - 1, x_peers[0], X_SUMS).wait_send()
    all_small(z_sums, z_chips - 1, z_peers[0], Z_SUMS).wait_send()
    all_small(inverses, y_chips - 1, y_peers[0], INVERSES).wait_send()
    pass_on().wait_send()
    all_small(totals, gc - 1, {"gc": 0}, TOTALS).wait_send()


def solution(mesh):
    gc, gr = mesh.shape["gc"], mesh.shape["gr"]

    def shards(weights, in_pattern, out_pattern):
        rows, cols = weights.shape
        br, bc = in_pattern.shape
        blk = rows // br
        tile = CAP * blk + CODE
        z_chips, y_chips = gc // X, gr // CORES
        dma = pltpu.SemaphoreType.DMA
        bf16, f32 = jnp.bfloat16, jnp.float32
        return pl.pallas_call(
            functools.partial(kernel, gc, gr, blk),
            out_shape=jax.ShapeDtypeStruct(weights.shape, weights.dtype),
            in_specs=[pl.BlockSpec(memory_space=pl.ANY)] * 3,
            out_specs=pl.BlockSpec(memory_space=pltpu.VMEM),
            scratch_shapes=[
                pltpu.VMEM((rows, cols), bf16),
                pltpu.SMEM((br, bc), jnp.int32),
                pltpu.SMEM((br, bc), jnp.int32),
                pltpu.VMEM((gc, P_ROWS, blk), bf16),
                pltpu.VMEM((gc, tile - P_ROWS, blk), bf16),
                pltpu.VMEM((gr, tile, blk), bf16),
                pltpu.VMEM((z_chips, X * rows, cols), bf16),
                pltpu.VMEM((z_chips, rows, X * rows), bf16),
                pltpu.VMEM((rows, cols), f32),
                pltpu.VMEM((X, bc, blk), f32),
                pltpu.VMEM((z_chips, bc, blk), f32),
                pltpu.VMEM((gr, bc, blk), f32),
                pltpu.VMEM((gc, bc, blk), f32),
                dma((2, z_chips // 2, 2 * (X + 1))),
                dma((2, X // 2, 2 * (z_chips + 1))),
                dma((2, y_chips // 2, 2)),
                dma((y_chips,)),
                dma((5,)),
                dma((8,)),
                dma((3,)),
                pltpu.SemaphoreType.REGULAR((RELAYS,)),
            ],
            compiler_params=pltpu.CompilerParams(
                collective_id=0, has_side_effects=True, vmem_limit_bytes=48 << 20
            ),
        )(weights, in_pattern, out_pattern)

    spec = P("gc", "gr")
    return jax.shard_map(shards, mesh=mesh, in_specs=(spec, spec, spec), out_specs=spec, check_vma=False)
```

```python
import functools

import jax
import jax.numpy as jnp
from jax import lax
from jax.experimental import pallas as pl
from jax.experimental.pallas import tpu as pltpu
from jax.sharding import PartitionSpec as P

MESH = pl.DeviceIdType.MESH
X = 4
CORES = 2
CAP = 4
CODE = 16
P_ROWS = 192
ROW, HOP, START, TAKE = 6.2e-3, 3.0, 0.1, 0.06

ALL = 2
RELAYS = 3
P_PIECES, Q_PIECES, Y_PIECES = (ALL,), (0, 1), (0, 1)


def slot_of(d, n):
    d %= n
    return 2 * d - 1 if 0 < d <= n // 2 else 2 * (n - d) if d else 0


def pieces(kind, item, z_chips):
    if kind == "y":
        return Y_PIECES
    return Q_PIECES if (kind == "z") == (item == (X if kind == "z" else z_chips)) else P_PIECES


def ring(kind, z_chips, y_chips):
    return {"x": X, "y": y_chips, "z": z_chips}[kind]


def goes(way, k, piece, n):
    return k < n // 2 or piece in (ALL, way)


def first_copies(z_chips):
    ways = range(2)
    order = (("z", X), ("x", z_chips), ("y", 0), ("z", 0), ("x", 0))
    return [(kind, way, 1, item, piece) for kind, item in order for piece in pieces(kind, item, z_chips) for way in ways]


def follow(step, done, z_chips, y_chips):
    kind, way, k, item, piece = step
    ways = range(2)
    n = ring(kind, z_chips, y_chips)
    steps = [(kind, way, k + 1, item, piece)] if k < n // 2 and goes(way, k + 1, piece, n) else []
    whole = k < n // 2 or piece != ALL or (kind, 1 - way, k, item, piece) in done
    came = slot_of(k if way else -k, n)
    if kind == "z" and item == X and whole:
        steps += [("x", d, 1, came, piece) for d in ways]
    if kind == "x" and item == z_chips and whole:
        steps += [("z", s, 1, came, piece) for s in ways]
    return steps


def halves(first, size):
    low = (size // 2 + CODE - 1) // CODE * CODE
    return (first, low), (first + low, size - low)


def plan(z_chips, y_chips, tile):
    row, hop, start, take = ROW, HOP, START, TAKE
    spread, dot, left = 0.5, 0.4, 0.25
    z_half, x_half, y_half = z_chips // 2, X // 2, y_chips // 2
    Q, PX = X, z_chips
    now, serial, free, arrivals, steps, done = 0.0, 0, {}, [], [], set()
    work = []

    def size(kind, way, k, item, piece):
        first = item != Q if kind == "z" else item == PX
        rows = tile if kind == "y" else P_ROWS if first else tile - P_ROWS
        if piece != ALL:
            return halves(0, rows)[piece][1]
        return halves(0, rows)[way][1] if k == ring(kind, z_chips, y_chips) // 2 else rows

    def arrive(when, step):
        nonlocal serial
        serial += 1
        arrivals.append((when, serial, step))

    def send(*step):
        nonlocal now
        now += start
        free[step[:2]] = max(now, free.get(step[:2], 0.0)) + size(*step) * row
        arrive(free[step[:2]] + hop, step)

    def small(kind, far, step):
        arrive(max(now, free.get((kind, 0), 0.0), free.get((kind, 1), 0.0)) + hop + far, step)

    def complete(dz):
        h = min(dz, z_chips - dz)
        parts = [("x", d, k, slot_of(dz, z_chips)) for d in range(2) for k in (1, 2)]
        if dz == 0:
            parts += [("x", d, k, PX) for d in range(2) for k in (1, 2)]
        else:
            ways = (0, 1) if dz == z_half else (1,) if dz < z_half else (0,)
            parts += [("z", s, h, item) for s in ways for item in range(X + 1)]
        need = {
            (kind, way, k, item, piece)
            for kind, way, k, item in parts
            for piece in pieces(kind, item, z_chips)
            if goes(way, k, piece, ring(kind, z_chips, y_chips))
        }
        return need <= done

    arrive(2.2, ("ready", 0))
    for step in first_copies(z_chips):
        send(*step)
    waiting = [dz for h in range(z_half + 1) for dz in dict.fromkeys((h, -h % z_chips))]
    scaled = False
    while arrivals or work:
        arrivals.sort()
        if not arrivals or (work and arrivals[0][0] > now):
            step = work.pop(0)
            steps.append(step)
            now += {"spread": spread, "dot": dot, "left": left}[step[0]]
            if step[0] == "spread":
                done.add(step)
        else:
            when, _, step = arrivals.pop(0)
            now = max(now, when) + take
            steps.append(step)
            done.add(step)
            kind = step[0]
            if kind in ("x", "y", "z"):
                for following in follow(step, done, z_chips, y_chips):
                    send(*following)
            elif kind == "ready":
                if step[1] + 1 < RELAYS:
                    arrive(now + 2.2, ("ready", step[1] + 1))
                if step[1] == 0:
                    small("x", 1.0, ("x_sums",))
            elif kind == "z_sums":
                small("y", 4.0, ("inverses",))
            if step in (("x_sums",), ("ready", RELAYS - 1)) and {("x_sums",), ("ready", RELAYS - 1)} <= done:
                steps.append(("column",))
                small("z", 4.0, ("z_sums",))
            if not scaled and not any(a[2][0] in ("y", "z_sums", "x_sums", "ready", "inverses") for a in arrivals):
                arrive(now + 2.0, ("all",))
                scaled = True
            if kind == "all":
                work[:0] = [("left", dy) for dy in range(y_chips)]
        for dz in list(waiting):
            if complete(dz):
                waiting.remove(dz)
                work.append(("spread", dz))
        if ("all",) in done:
            for dz in range(z_chips):
                if ("spread", dz) in done and ("dot", dz) not in done:
                    done.add(("dot", dz))
                    work.append(("dot", dz))
    return steps, now


def kernel(
    gc, gr, blk,
    w_hbm, ip_hbm, op_hbm, o_ref,
    w_ref, ip_ref, op_ref, pbuf, qbuf, abuf, bdense, adense, acc, x_sums, z_sums, inverses, totals,
    z_recv, x_recv, y_recv, sib_recv, small_recv, send_sem, local_sem, ready_sem,
):
    br, bc = ip_ref.shape
    z_chips, y_chips = gc // X, gr // CORES
    x_half, y_half, z_half = X // 2, y_chips // 2, z_chips // 2
    data = CAP * blk
    tile = data + CODE
    f32, bf16 = jnp.float32, jnp.bfloat16

    me = lax.axis_index("gc")
    mine = lax.axis_index("gr")
    x, z = lax.rem(me, X), lax.div(me, X)
    core, y = lax.rem(mine, CORES), lax.div(mine, CORES)

    def at(dx, dz):
        return lax.rem(z + (dz + z_chips), z_chips) * X + lax.rem(x + (dx + X), X)

    def at_y(dy, c):
        return lax.rem(y + (dy + y_chips), y_chips) * CORES + c

    barrier = pltpu.get_barrier_semaphore()
    x_peers = [{"gc": at(i, 0)} for i in range(1, X)]
    z_peers = [{"gc": at(0, i)} for i in range(1, z_chips)]
    y_peers = [{"gr": at_y(i, core)} for i in range(1, y_chips)]
    other_core = {"gr": at_y(0, 1 - core)}
    nearest = [{"gc": at(1, 0)}, {"gc": at(-1, 0)}, {"gc": at(0, 1)}, {"gc": at(0, -1)}, {"gr": at_y(1, core)}, {"gr": at_y(-1, core)}]
    greeted = nearest + [other_core]
    for peer in greeted:
        pl.semaphore_signal(barrier, inc=1, device_id=peer, device_id_type=MESH)
    loads = [
        pltpu.make_async_copy(src, dst, local_sem.at[i])
        for i, (src, dst) in enumerate(((w_hbm, w_ref), (ip_hbm, ip_ref), (op_hbm, op_ref)))
    ]
    for load in loads:
        load.start()
    for load in loads[:2]:
        load.wait()

    spots = br * bc
    on = [(ip_ref[p // bc, p % bc] > 0).astype(jnp.int32) for p in range(spots)]
    spare = CAP - sum(on)
    count = jnp.int32(0)
    place = [jnp.int32(0)] * CAP
    for p in range(spots):
        filler = jnp.logical_and(on[p] == 0, spare > 0).astype(jnp.int32)
        spare = spare - filler
        used = on[p] + filler
        for s in range(CAP):
            place[s] = place[s] + jnp.where(count == s, used, 0) * p
        count = count + used

    def reach(p):
        return range(max(0, p - (spots - CAP)), min(CAP - 1, p) + 1)

    def block_of(p):
        r, c = p // bc, p % bc
        return w_ref[r * blk : (r + 1) * blk, c * blk : (c + 1) * blk]

    def put(first, block):
        size = block.shape[0]
        abuf[0, first : first + size, :] = block
        cut = min(max(P_ROWS - first, 0), size)
        if cut > 0:
            pbuf[0, first : first + cut, :] = block[:cut]
        if cut < size:
            qbuf[0, first + cut - P_ROWS : first + size - P_ROWS, :] = block[cut:]

    code_row = lax.broadcasted_iota(jnp.int32, (CODE, blk), 0)
    codes = jnp.zeros((CODE, blk), f32)
    for s in range(CAP):
        slot = sum(
            block_of(p) * jnp.full((1, blk), jnp.where(place[s] == p, on[p], 0).astype(f32)).astype(bf16)
            for p in range(s, s + spots - CAP + 1)
        )
        put(s * blk, slot)
        codes = jnp.where(code_row == s, place[s].astype(f32), codes)
    put(data, codes.astype(bf16))

    pl.semaphore_wait(barrier, len(greeted))

    down = {"z": [{"gc": at(0, 1)}, {"gc": at(0, -1)}], "x": [{"gc": at(1, 0)}, {"gc": at(-1, 0)}],
            "y": [{"gr": at_y(1, core)}, {"gr": at_y(-1, core)}]}
    landed = {"z": z_recv, "x": x_recv, "y": y_recv}
    sent = {"p": send_sem.at[0], "q": send_sem.at[7], "a": send_sem.at[1]}
    which = {"p": pbuf, "q": qbuf, "a": abuf}

    def move(name, src, dst, count, rows, sem, peer):
        ref, (first, size) = which[name], rows
        return pltpu.make_async_remote_copy(
            src_ref=ref.at[src : src + count, first : first + size, :],
            dst_ref=ref.at[dst : dst + count, first : first + size, :],
            send_sem=sent[name], recv_sem=sem, device_id=peer, device_id_type=MESH,
        )

    def link(kind, way, k, item, piece):
        sign = 1 - 2 * way
        n = ring(kind, z_chips, y_chips)
        here, there = slot_of(-sign * (k - 1), n), slot_of(-sign * k, n)
        whole = {"p": (0, P_ROWS), "q": (0, tile - P_ROWS), "a": (0, tile)}
        if kind == "y":
            name, src, dst = "a", here, there
        elif kind == "z":
            name = "q" if item == X else "p"
            src, dst = (here, there) if item == X else (here * X + item, there * X + item)
        else:
            name = "p" if item == z_chips else "q"
            src, dst = (here, there) if item == z_chips else (here * z_chips + item, there * z_chips + item)
        rows = whole[name]
        if piece != ALL or k == n // 2:
            rows = halves(*rows)[way if piece == ALL else piece]
        sem = landed[kind].at[way, k - 1, 2 * item + piece % 2]
        return move(name, src, dst, 1, rows, sem, down[kind][way])

    def sib_copy(dy):
        i = slot_of(dy, y_chips)
        return move("a", i, y_chips + i, 1, (0, tile), sib_recv.at[i], other_core)

    def small(ref, index, peer, k):
        return pltpu.make_async_remote_copy(
            src_ref=ref.at[0], dst_ref=ref.at[index], send_sem=send_sem.at[k], recv_sem=small_recv.at[k - 2],
            device_id=peer, device_id_type=MESH,
        )

    def all_small(ref, n, peer, k):
        view = ref.at[pl.ds(0, n)]
        return pltpu.make_async_remote_copy(
            src_ref=view, dst_ref=view, send_sem=send_sem.at[k], recv_sem=small_recv.at[k - 2],
            device_id=peer, device_id_type=MESH,
        )

    X_SUMS, Z_SUMS, INVERSES, TOTALS, PASSED = 2, 3, 4, 5, 6

    def pass_on():
        return pltpu.make_async_remote_copy(
            src_ref=inverses.at[pl.ds(0, y_chips)], dst_ref=inverses.at[pl.ds(y_chips, y_chips)],
            send_sem=send_sem.at[PASSED], recv_sem=small_recv.at[PASSED - 2],
            device_id=other_core, device_id_type=MESH,
        )

    def spread(load, dst, r_base, c_base, inverse=None):
        codes = load(data, CODE).astype(f32)
        places = [codes[s : s + 1, :] for s in range(CAP)]
        slots = [load(s * blk, blk) for s in range(CAP)]
        if inverse is not None:
            for s in range(CAP):
                factor = sum(
                    inverse[c : c + 1, :] * sum((places[s] == float(r * bc + c)).astype(f32) for r in range(br))
                    for c in range(bc)
                )
                slots[s] = (slots[s].astype(f32) * factor).astype(bf16)
        for p in range(spots):
            block = sum(slots[s] * (places[s] == float(p)).astype(f32).astype(bf16) for s in reach(p))
            r, c = p // bc, p % bc
            dst[pl.ds(r_base + r * blk, blk), pl.ds(c_base + c * blk, blk)] = block

    def left(dy):
        zz = lax.rem(y + dy, y_chips)
        for other in range(CORES):
            i = other * y_chips + slot_of(dy, y_chips)
            c_base = pl.multiple_of((core if other == 0 else 1 - core) * (bc * blk), blk)
            spread(lambda first, size, i=i: abuf[i, first : first + size, :], adense.at[zz], 0, c_base, inverses[i])

    def right(dz):
        zs = slot_of(dz, z_chips)

        @pl.loop(0, X)
        def _(i):
            def load(first, size):
                cut = min(max(P_ROWS - first, 0), size)
                parts = []
                if cut > 0:
                    parts.append(pbuf[zs * X + i, first : first + cut, :])
                if cut < size:
                    parts.append(qbuf[i * z_chips + zs, first + cut - P_ROWS : first + size - P_ROWS, :])
                return parts[0] if len(parts) == 1 else jnp.concatenate(parts, axis=0)

            dx = i + jnp.where(i == 2, 1, 0) - jnp.where(i == 3, 1, 0)
            spread(load, bdense.at[zs], pl.multiple_of(lax.rem(x + dx, X) * (br * blk), blk), 0)

    def relay(i):
        for peer in nearest:
            pl.semaphore_signal(ready_sem.at[i], inc=1, device_id=peer, device_id_type=MESH)

    relay(0)
    for step in first_copies(z_chips):
        link(*step).start()
    sib_copy(0).start()

    for c in range(bc):
        total = jnp.zeros((1, blk), f32)
        for r in range(br):
            block = block_of(r * bc + c).astype(f32)
            total += jnp.sum(block, axis=0, keepdims=True) * on[r * bc + c].astype(f32)
        x_sums[0, c : c + 1, :] = total

    taken = set()
    first = True
    for step in plan(z_chips, y_chips, tile)[0]:
        kind = step[0]
        if kind in landed:
            link(*step).wait_recv()
            for following in follow(step, taken, z_chips, y_chips):
                link(*following).start()
            if kind == "y":
                _, way, k, _, piece = step
                if ("y", way if k < y_half else 1 - way, k, 0, 1 - piece) in taken:
                    sib_copy(k if way else -k).start()
        elif kind == "ready":
            pl.semaphore_wait(ready_sem.at[step[1]], len(nearest))
            if step[1] + 1 < RELAYS:
                relay(step[1] + 1)
            if step[1] == 0:
                for i, peer in enumerate(x_peers):
                    small(x_sums, X - 1 - i, peer, X_SUMS).start()
        elif kind == "x_sums":
            all_small(x_sums, X - 1, x_peers[0], X_SUMS).wait_recv()
            z_sums[0] = jnp.sum(x_sums[...], axis=0)
        elif kind == "column":
            for i, peer in enumerate(z_peers):
                small(z_sums, z_chips - 1 - i, peer, Z_SUMS).start()
        elif kind == "z_sums":
            all_small(z_sums, z_chips - 1, z_peers[0], Z_SUMS).wait_recv()
            inverses[0] = 1.0 / jnp.sum(z_sums[...], axis=0)
            for i, peer in enumerate(y_peers):
                small(inverses, slot_of(-1 - i, y_chips), peer, INVERSES).start()
        elif kind == "inverses":
            all_small(inverses, y_chips - 1, y_peers[0], INVERSES).wait_recv()
            pass_on().start()
        elif kind == "all":
            for dy in range(y_chips):
                sib_copy(dy).wait_recv()
            pass_on().wait_recv()
        elif kind == "left":
            left(step[1])
        elif kind == "spread":
            right(step[1])
        elif kind == "dot":
            zz = lax.rem(z + step[1], z_chips)
            term = jnp.dot(adense[zz], bdense[slot_of(step[1], z_chips)], preferred_element_type=f32)
            acc[...] = term if first else acc[...] + term
            first = False
        taken.add(step)

    loads[2].wait()
    for c in range(bc):
        total = jnp.zeros((1, blk), f32)
        for r in range(br):
            block = acc[r * blk : (r + 1) * blk, c * blk : (c + 1) * blk] * op_ref[r, c].astype(f32)
            block = block * block
            acc[r * blk : (r + 1) * blk, c * blk : (c + 1) * blk] = block
            total += jnp.sum(block, axis=0, keepdims=True)
        totals[0, c : c + 1, :] = total
    far_first = sorted(
        ((dx, dz) for dx in range(X) for dz in range(z_chips) if dx or dz),
        key=lambda p: -(min(p[0], X - p[0]) + min(p[1], z_chips - p[1])),
    )
    for dx, dz in far_first:
        small(totals, -dz % z_chips * X + -dx % X, {"gc": at(dx, dz)}, TOTALS).start()
    all_small(totals, gc - 1, {"gc": 0}, TOTALS).wait_recv()
    factor = float(gc * br * blk) / jnp.sum(totals[...], axis=0)
    for c in range(bc):
        o_ref[:, c * blk : (c + 1) * blk] = (acc[:, c * blk : (c + 1) * blk] * factor[c : c + 1, :]).astype(bf16)

    neighbour = down["x"][0]
    move("p", 0, 0, gc - 1, (0, P_ROWS), x_recv.at[0, 0, 0], neighbour).wait_send()
    move("q", 0, 0, gc - 1, (0, tile - P_ROWS), x_recv.at[0, 0, 0], neighbour).wait_send()
    move("a", 0, 0, gr - 1, (0, tile), sib_recv.at[0], other_core).wait_send()
    all_small(x_sums, X - 1, x_peers[0], X_SUMS).wait_send()
    all_small(z_sums, z_chips - 1, z_peers[0], Z_SUMS).wait_send()
    all_small(inverses, y_chips - 1, y_peers[0], INVERSES).wait_send()
    pass_on().wait_send()
    all_small(totals, gc - 1, {"gc": 0}, TOTALS).wait_send()


def solution(mesh):
    gc, gr = mesh.shape["gc"], mesh.shape["gr"]

    def shards(weights, in_pattern, out_pattern):
        rows, cols = weights.shape
        br, bc = in_pattern.shape
        blk = rows // br
        tile = CAP * blk + CODE
        z_chips, y_chips = gc // X, gr // CORES
        dma = pltpu.SemaphoreType.DMA
        bf16, f32 = jnp.bfloat16, jnp.float32
        return pl.pallas_call(
            functools.partial(kernel, gc, gr, blk),
            out_shape=jax.ShapeDtypeStruct(weights.shape, weights.dtype),
            in_specs=[pl.BlockSpec(memory_space=pl.ANY)] * 3,
            out_specs=pl.BlockSpec(memory_space=pltpu.VMEM),
            scratch_shapes=[
                pltpu.VMEM((rows, cols), bf16),
                pltpu.SMEM((br, bc), jnp.int32),
                pltpu.SMEM((br, bc), jnp.int32),
                pltpu.VMEM((gc, P_ROWS, blk), bf16),
                pltpu.VMEM((gc, tile - P_ROWS, blk), bf16),
                pltpu.VMEM((gr, tile, blk), bf16),
                pltpu.VMEM((z_chips, X * rows, cols), bf16),
                pltpu.VMEM((z_chips, rows, X * rows), bf16),
                pltpu.VMEM((rows, cols), f32),
                pltpu.VMEM((X, bc, blk), f32),
                pltpu.VMEM((z_chips, bc, blk), f32),
                pltpu.VMEM((gr, bc, blk), f32),
                pltpu.VMEM((gc, bc, blk), f32),
                dma((2, z_chips // 2, 2 * (X + 1))),
                dma((2, X // 2, 2 * (z_chips + 1))),
                dma((2, y_chips // 2, 2)),
                dma((y_chips,)),
                dma((5,)),
                dma((8,)),
                dma((3,)),
                pltpu.SemaphoreType.REGULAR((RELAYS,)),
            ],
            compiler_params=pltpu.CompilerParams(
                collective_id=0, has_side_effects=True, vmem_limit_bytes=48 << 20
            ),
        )(weights, in_pattern, out_pattern)

    spec = P("gc", "gr")
    return jax.shard_map(shards, mesh=mesh, in_specs=(spec, spec, spec), out_specs=spec, check_vma=False)
```

```python
import functools

import jax
import jax.numpy as jnp
from jax import lax
from jax.experimental import pallas as pl
from jax.experimental.pallas import tpu as pltpu
from jax.sharding import PartitionSpec as P

MESH = pl.DeviceIdType.MESH
X = 4
CORES = 2
CAP = 4
CODE = 16
P_ROWS = 192
ROW, HOP, START, TAKE = 6.2e-3, 3.0, 0.1, 0.06

ALL = 2
RELAYS = 3
P_PIECES, Q_PIECES, Y_PIECES = (ALL,), (0, 1), (0, 1)


def slot_of(d, n):
    d %= n
    return 2 * d - 1 if 0 < d <= n // 2 else 2 * (n - d) if d else 0


def pieces(kind, item, z_chips):
    if kind == "y":
        return Y_PIECES
    return Q_PIECES if (kind == "z") == (item == (X if kind == "z" else z_chips)) else P_PIECES


def ring(kind, z_chips, y_chips):
    return {"x": X, "y": y_chips, "z": z_chips}[kind]


def goes(way, k, piece, n):
    return k < n // 2 or piece in (ALL, way)


def first_copies(z_chips):
    ways = range(2)
    order = (("z", X), ("x", z_chips), ("y", 0), ("z", 0), ("x", 0))
    return [(kind, way, 1, item, piece) for kind, item in order for piece in pieces(kind, item, z_chips) for way in ways]


def follow(step, done, z_chips, y_chips):
    kind, way, k, item, piece = step
    ways = range(2)
    n = ring(kind, z_chips, y_chips)
    steps = [(kind, way, k + 1, item, piece)] if k < n // 2 and goes(way, k + 1, piece, n) else []
    whole = k < n // 2 or piece != ALL or (kind, 1 - way, k, item, piece) in done
    came = slot_of(k if way else -k, n)
    if kind == "z" and item == X and whole:
        steps += [("x", d, 1, came, piece) for d in ways]
    if kind == "x" and item == z_chips and whole:
        steps += [("z", s, 1, came, piece) for s in ways]
    return steps


def halves(first, size):
    low = (size // 2 + CODE - 1) // CODE * CODE
    return (first, low), (first + low, size - low)


def plan(z_chips, y_chips, tile):
    row, hop, start, take = ROW, HOP, START, TAKE
    spread, dot, left = 0.7, 0.6, 0.4
    z_half, x_half, y_half = z_chips // 2, X // 2, y_chips // 2
    Q, PX = X, z_chips
    now, serial, free, arrivals, steps, done = 0.0, 0, {}, [], [], set()
    work = []

    def size(kind, way, k, item, piece):
        first = item != Q if kind == "z" else item == PX
        rows = tile if kind == "y" else P_ROWS if first else tile - P_ROWS
        if piece != ALL:
            return halves(0, rows)[piece][1]
        return halves(0, rows)[way][1] if k == ring(kind, z_chips, y_chips) // 2 else rows

    def arrive(when, step):
        nonlocal serial
        serial += 1
        arrivals.append((when, serial, step))

    def send(*step):
        nonlocal now
        now += start
        free[step[:2]] = max(now, free.get(step[:2], 0.0)) + size(*step) * row
        arrive(free[step[:2]] + hop, step)

    def small(kind, far, step):
        arrive(max(now, free.get((kind, 0), 0.0), free.get((kind, 1), 0.0)) + hop + far, step)

    def complete(dz):
        h = min(dz, z_chips - dz)
        parts = [("x", d, k, slot_of(dz, z_chips)) for d in range(2) for k in (1, 2)]
        if dz == 0:
            parts += [("x", d, k, PX) for d in range(2) for k in (1, 2)]
        else:
            ways = (0, 1) if dz == z_half else (1,) if dz < z_half else (0,)
            parts += [("z", s, h, item) for s in ways for item in range(X + 1)]
        need = {
            (kind, way, k, item, piece)
            for kind, way, k, item in parts
            for piece in pieces(kind, item, z_chips)
            if goes(way, k, piece, ring(kind, z_chips, y_chips))
        }
        return need <= done

    arrive(2.2, ("ready", 0))
    for step in first_copies(z_chips):
        send(*step)
    waiting = [dz for h in range(z_half + 1) for dz in dict.fromkeys((h, -h % z_chips))]
    scaled = False
    while arrivals or work:
        arrivals.sort()
        if not arrivals or (work and arrivals[0][0] > now):
            step = work.pop(0)
            steps.append(step)
            now += {"spread": spread, "dot": dot, "left": left}[step[0]]
            if step[0] == "spread":
                done.add(step)
        else:
            when, _, step = arrivals.pop(0)
            now = max(now, when) + take
            steps.append(step)
            done.add(step)
            kind = step[0]
            if kind in ("x", "y", "z"):
                for following in follow(step, done, z_chips, y_chips):
                    send(*following)
            elif kind == "ready":
                if step[1] + 1 < RELAYS:
                    arrive(now + 2.2, ("ready", step[1] + 1))
                if step[1] == 0:
                    small("x", 1.0, ("x_sums",))
            elif kind == "z_sums":
                small("y", 4.0, ("inverses",))
            if step in (("x_sums",), ("ready", RELAYS - 1)) and {("x_sums",), ("ready", RELAYS - 1)} <= done:
                steps.append(("column",))
                small("z", 4.0, ("z_sums",))
            if not scaled and not any(a[2][0] in ("y", "z_sums", "x_sums", "ready", "inverses") for a in arrivals):
                arrive(now + 2.0, ("all",))
                scaled = True
            if kind == "all":
                work[:0] = [("left", dy) for dy in range(y_chips)]
        for dz in list(waiting):
            if complete(dz):
                waiting.remove(dz)
                work.append(("spread", dz))
        if ("all",) in done:
            for dz in range(z_chips):
                if ("spread", dz) in done and ("dot", dz) not in done:
                    done.add(("dot", dz))
                    work.append(("dot", dz))
    return steps, now


def kernel(
    gc, gr, blk,
    w_hbm, ip_hbm, op_hbm, o_ref,
    w_ref, ip_ref, op_ref, pbuf, qbuf, abuf, bdense, adense, acc, x_sums, z_sums, inverses, totals,
    z_recv, x_recv, y_recv, sib_recv, small_recv, send_sem, local_sem, ready_sem,
):
    br, bc = ip_ref.shape
    z_chips, y_chips = gc // X, gr // CORES
    x_half, y_half, z_half = X // 2, y_chips // 2, z_chips // 2
    data = CAP * blk
    tile = data + CODE
    f32, bf16 = jnp.float32, jnp.bfloat16

    me = lax.axis_index("gc")
    mine = lax.axis_index("gr")
    x, z = lax.rem(me, X), lax.div(me, X)
    core, y = lax.rem(mine, CORES), lax.div(mine, CORES)

    def at(dx, dz):
        return lax.rem(z + (dz + z_chips), z_chips) * X + lax.rem(x + (dx + X), X)

    def at_y(dy, c):
        return lax.rem(y + (dy + y_chips), y_chips) * CORES + c

    barrier = pltpu.get_barrier_semaphore()
    x_peers = [{"gc": at(i, 0)} for i in range(1, X)]
    z_peers = [{"gc": at(0, i)} for i in range(1, z_chips)]
    y_peers = [{"gr": at_y(i, core)} for i in range(1, y_chips)]
    other_core = {"gr": at_y(0, 1 - core)}
    nearest = [{"gc": at(1, 0)}, {"gc": at(-1, 0)}, {"gc": at(0, 1)}, {"gc": at(0, -1)}, {"gr": at_y(1, core)}, {"gr": at_y(-1, core)}]
    greeted = nearest + [other_core]
    for peer in greeted:
        pl.semaphore_signal(barrier, inc=1, device_id=peer, device_id_type=MESH)
    loads = [
        pltpu.make_async_copy(src, dst, local_sem.at[i])
        for i, (src, dst) in enumerate(((w_hbm, w_ref), (ip_hbm, ip_ref), (op_hbm, op_ref)))
    ]
    for load in loads:
        load.start()
    for load in loads[:2]:
        load.wait()

    spots = br * bc
    on = [(ip_ref[p // bc, p % bc] > 0).astype(jnp.int32) for p in range(spots)]
    spare = CAP - sum(on)
    count = jnp.int32(0)
    place = [jnp.int32(0)] * CAP
    for p in range(spots):
        filler = jnp.logical_and(on[p] == 0, spare > 0).astype(jnp.int32)
        spare = spare - filler
        used = on[p] + filler
        for s in range(CAP):
            place[s] = place[s] + jnp.where(count == s, used, 0) * p
        count = count + used

    def reach(p):
        return range(max(0, p - (spots - CAP)), min(CAP - 1, p) + 1)

    def block_of(p):
        r, c = p // bc, p % bc
        return w_ref[r * blk : (r + 1) * blk, c * blk : (c + 1) * blk]

    def put(first, block):
        size = block.shape[0]
        abuf[0, first : first + size, :] = block
        cut = min(max(P_ROWS - first, 0), size)
        if cut > 0:
            pbuf[0, first : first + cut, :] = block[:cut]
        if cut < size:
            qbuf[0, first + cut - P_ROWS : first + size - P_ROWS, :] = block[cut:]

    code_row = lax.broadcasted_iota(jnp.int32, (CODE, blk), 0)
    codes = jnp.zeros((CODE, blk), f32)
    for s in range(CAP):
        slot = sum(
            block_of(p) * jnp.full((1, blk), jnp.where(place[s] == p, on[p], 0).astype(f32)).astype(bf16)
            for p in range(s, s + spots - CAP + 1)
        )
        put(s * blk, slot)
        codes = jnp.where(code_row == s, place[s].astype(f32), codes)
    put(data, codes.astype(bf16))

    pl.semaphore_wait(barrier, len(greeted))

    down = {"z": [{"gc": at(0, 1)}, {"gc": at(0, -1)}], "x": [{"gc": at(1, 0)}, {"gc": at(-1, 0)}],
            "y": [{"gr": at_y(1, core)}, {"gr": at_y(-1, core)}]}
    landed = {"z": z_recv, "x": x_recv, "y": y_recv}
    sent = {"p": send_sem.at[0], "q": send_sem.at[7], "a": send_sem.at[1]}
    which = {"p": pbuf, "q": qbuf, "a": abuf}

    def move(name, src, dst, count, rows, sem, peer):
        ref, (first, size) = which[name], rows
        return pltpu.make_async_remote_copy(
            src_ref=ref.at[src : src + count, first : first + size, :],
            dst_ref=ref.at[dst : dst + count, first : first + size, :],
            send_sem=sent[name], recv_sem=sem, device_id=peer, device_id_type=MESH,
        )

    def link(kind, way, k, item, piece):
        sign = 1 - 2 * way
        n = ring(kind, z_chips, y_chips)
        here, there = slot_of(-sign * (k - 1), n), slot_of(-sign * k, n)
        whole = {"p": (0, P_ROWS), "q": (0, tile - P_ROWS), "a": (0, tile)}
        if kind == "y":
            name, src, dst = "a", here, there
        elif kind == "z":
            name = "q" if item == X else "p"
            src, dst = (here, there) if item == X else (here * X + item, there * X + item)
        else:
            name = "p" if item == z_chips else "q"
            src, dst = (here, there) if item == z_chips else (here * z_chips + item, there * z_chips + item)
        rows = whole[name]
        if piece != ALL or k == n // 2:
            rows = halves(*rows)[way if piece == ALL else piece]
        sem = landed[kind].at[way, k - 1, 2 * item + piece % 2]
        return move(name, src, dst, 1, rows, sem, down[kind][way])

    def sib_copy(dy):
        i = slot_of(dy, y_chips)
        return move("a", i, y_chips + i, 1, (0, tile), sib_recv.at[i], other_core)

    def small(ref, index, peer, k):
        return pltpu.make_async_remote_copy(
            src_ref=ref.at[0], dst_ref=ref.at[index], send_sem=send_sem.at[k], recv_sem=small_recv.at[k - 2],
            device_id=peer, device_id_type=MESH,
        )

    def all_small(ref, n, peer, k):
        view = ref.at[pl.ds(0, n)]
        return pltpu.make_async_remote_copy(
            src_ref=view, dst_ref=view, send_sem=send_sem.at[k], recv_sem=small_recv.at[k - 2],
            device_id=peer, device_id_type=MESH,
        )

    X_SUMS, Z_SUMS, INVERSES, TOTALS, PASSED = 2, 3, 4, 5, 6

    def pass_on():
        return pltpu.make_async_remote_copy(
            src_ref=inverses.at[pl.ds(0, y_chips)], dst_ref=inverses.at[pl.ds(y_chips, y_chips)],
            send_sem=send_sem.at[PASSED], recv_sem=small_recv.at[PASSED - 2],
            device_id=other_core, device_id_type=MESH,
        )

    def spread(load, dst, r_base, c_base, inverse=None):
        codes = load(data, CODE).astype(f32)
        places = [codes[s : s + 1, :] for s in range(CAP)]
        slots = [load(s * blk, blk) for s in range(CAP)]
        if inverse is not None:
            for s in range(CAP):
                factor = sum(
                    inverse[c : c + 1, :] * sum((places[s] == float(r * bc + c)).astype(f32) for r in range(br))
                    for c in range(bc)
                )
                slots[s] = (slots[s].astype(f32) * factor).astype(bf16)
        for p in range(spots):
            block = sum(slots[s] * (places[s] == float(p)).astype(f32).astype(bf16) for s in reach(p))
            r, c = p // bc, p % bc
            dst[pl.ds(r_base + r * blk, blk), pl.ds(c_base + c * blk, blk)] = block

    def left(dy):
        zz = lax.rem(y + dy, y_chips)
        for other in range(CORES):
            i = other * y_chips + slot_of(dy, y_chips)
            c_base = pl.multiple_of((core if other == 0 else 1 - core) * (bc * blk), blk)
            spread(lambda first, size, i=i: abuf[i, first : first + size, :], adense.at[zz], 0, c_base, inverses[i])

    def right(dz):
        zs = slot_of(dz, z_chips)

        @pl.loop(0, X)
        def _(i):
            def load(first, size):
                cut = min(max(P_ROWS - first, 0), size)
                parts = []
                if cut > 0:
                    parts.append(pbuf[zs * X + i, first : first + cut, :])
                if cut < size:
                    parts.append(qbuf[i * z_chips + zs, first + cut - P_ROWS : first + size - P_ROWS, :])
                return parts[0] if len(parts) == 1 else jnp.concatenate(parts, axis=0)

            dx = i + jnp.where(i == 2, 1, 0) - jnp.where(i == 3, 1, 0)
            spread(load, bdense.at[zs], pl.multiple_of(lax.rem(x + dx, X) * (br * blk), blk), 0)

    def relay(i):
        for peer in nearest:
            pl.semaphore_signal(ready_sem.at[i], inc=1, device_id=peer, device_id_type=MESH)

    relay(0)
    for step in first_copies(z_chips):
        link(*step).start()
    sib_copy(0).start()

    for c in range(bc):
        total = jnp.zeros((1, blk), f32)
        for r in range(br):
            block = block_of(r * bc + c).astype(f32)
            total += jnp.sum(block, axis=0, keepdims=True) * on[r * bc + c].astype(f32)
        x_sums[0, c : c + 1, :] = total

    taken = set()
    first = True
    for step in plan(z_chips, y_chips, tile)[0]:
        kind = step[0]
        if kind in landed:
            link(*step).wait_recv()
            for following in follow(step, taken, z_chips, y_chips):
                link(*following).start()
            if kind == "y":
                _, way, k, _, piece = step
                if ("y", way if k < y_half else 1 - way, k, 0, 1 - piece) in taken:
                    sib_copy(k if way else -k).start()
        elif kind == "ready":
            pl.semaphore_wait(ready_sem.at[step[1]], len(nearest))
            if step[1] + 1 < RELAYS:
                relay(step[1] + 1)
            if step[1] == 0:
                for i, peer in enumerate(x_peers):
                    small(x_sums, X - 1 - i, peer, X_SUMS).start()
        elif kind == "x_sums":
            all_small(x_sums, X - 1, x_peers[0], X_SUMS).wait_recv()
            z_sums[0] = jnp.sum(x_sums[...], axis=0)
        elif kind == "column":
            for i, peer in enumerate(z_peers):
                small(z_sums, z_chips - 1 - i, peer, Z_SUMS).start()
        elif kind == "z_sums":
            all_small(z_sums, z_chips - 1, z_peers[0], Z_SUMS).wait_recv()
            inverses[0] = 1.0 / jnp.sum(z_sums[...], axis=0)
            for i, peer in enumerate(y_peers):
                small(inverses, slot_of(-1 - i, y_chips), peer, INVERSES).start()
        elif kind == "inverses":
            all_small(inverses, y_chips - 1, y_peers[0], INVERSES).wait_recv()
            pass_on().start()
        elif kind == "all":
            for dy in range(y_chips):
                sib_copy(dy).wait_recv()
            pass_on().wait_recv()
        elif kind == "left":
            left(step[1])
        elif kind == "spread":
            right(step[1])
        elif kind == "dot":
            zz = lax.rem(z + step[1], z_chips)
            term = jnp.dot(adense[zz], bdense[slot_of(step[1], z_chips)], preferred_element_type=f32)
            acc[...] = term if first else acc[...] + term
            first = False
        taken.add(step)

    loads[2].wait()
    for c in range(bc):
        total = jnp.zeros((1, blk), f32)
        for r in range(br):
            block = acc[r * blk : (r + 1) * blk, c * blk : (c + 1) * blk] * op_ref[r, c].astype(f32)
            block = block * block
            acc[r * blk : (r + 1) * blk, c * blk : (c + 1) * blk] = block
            total += jnp.sum(block, axis=0, keepdims=True)
        totals[0, c : c + 1, :] = total
    far_first = sorted(
        ((dx, dz) for dx in range(X) for dz in range(z_chips) if dx or dz),
        key=lambda p: -(min(p[0], X - p[0]) + min(p[1], z_chips - p[1])),
    )
    for dx, dz in far_first:
        small(totals, -dz % z_chips * X + -dx % X, {"gc": at(dx, dz)}, TOTALS).start()
    all_small(totals, gc - 1, {"gc": 0}, TOTALS).wait_recv()
    factor = float(gc * br * blk) / jnp.sum(totals[...], axis=0)
    for c in range(bc):
        o_ref[:, c * blk : (c + 1) * blk] = (acc[:, c * blk : (c + 1) * blk] * factor[c : c + 1, :]).astype(bf16)

    neighbour = down["x"][0]
    move("p", 0, 0, gc - 1, (0, P_ROWS), x_recv.at[0, 0, 0], neighbour).wait_send()
    move("q", 0, 0, gc - 1, (0, tile - P_ROWS), x_recv.at[0, 0, 0], neighbour).wait_send()
    move("a", 0, 0, gr - 1, (0, tile), sib_recv.at[0], other_core).wait_send()
    all_small(x_sums, X - 1, x_peers[0], X_SUMS).wait_send()
    all_small(z_sums, z_chips - 1, z_peers[0], Z_SUMS).wait_send()
    all_small(inverses, y_chips - 1, y_peers[0], INVERSES).wait_send()
    pass_on().wait_send()
    all_small(totals, gc - 1, {"gc": 0}, TOTALS).wait_send()


def solution(mesh):
    gc, gr = mesh.shape["gc"], mesh.shape["gr"]

    def shards(weights, in_pattern, out_pattern):
        rows, cols = weights.shape
        br, bc = in_pattern.shape
        blk = rows // br
        tile = CAP * blk + CODE
        z_chips, y_chips = gc // X, gr // CORES
        dma = pltpu.SemaphoreType.DMA
        bf16, f32 = jnp.bfloat16, jnp.float32
        return pl.pallas_call(
            functools.partial(kernel, gc, gr, blk),
            out_shape=jax.ShapeDtypeStruct(weights.shape, weights.dtype),
            in_specs=[pl.BlockSpec(memory_space=pl.ANY)] * 3,
            out_specs=pl.BlockSpec(memory_space=pltpu.VMEM),
            scratch_shapes=[
                pltpu.VMEM((rows, cols), bf16),
                pltpu.SMEM((br, bc), jnp.int32),
                pltpu.SMEM((br, bc), jnp.int32),
                pltpu.VMEM((gc, P_ROWS, blk), bf16),
                pltpu.VMEM((gc, tile - P_ROWS, blk), bf16),
                pltpu.VMEM((gr, tile, blk), bf16),
                pltpu.VMEM((z_chips, X * rows, cols), bf16),
                pltpu.VMEM((z_chips, rows, X * rows), bf16),
                pltpu.VMEM((rows, cols), f32),
                pltpu.VMEM((X, bc, blk), f32),
                pltpu.VMEM((z_chips, bc, blk), f32),
                pltpu.VMEM((gr, bc, blk), f32),
                pltpu.VMEM((gc, bc, blk), f32),
                dma((2, z_chips // 2, 2 * (X + 1))),
                dma((2, X // 2, 2 * (z_chips + 1))),
                dma((2, y_chips // 2, 2)),
                dma((y_chips,)),
                dma((5,)),
                dma((8,)),
                dma((3,)),
                pltpu.SemaphoreType.REGULAR((RELAYS,)),
            ],
            compiler_params=pltpu.CompilerParams(
                collective_id=0, has_side_effects=True, vmem_limit_bytes=48 << 20
            ),
        )(weights, in_pattern, out_pattern)

    spec = P("gc", "gr")
    return jax.shard_map(shards, mesh=mesh, in_specs=(spec, spec, spec), out_specs=spec, check_vma=False)
```
